128 devices in a mesh: grp: 2 (over y_hi), dev: 64 (over x, z, y_lo, core).
Axes of the slice: x: 4, y: 4 (y_hi: 2, y_lo: 2; y = y_hi * 2 + y_lo), z: 4, core: 2. Of those that a mesh axis runs over, the one named last changes fastest.
Arguments:
- multipoles: float32 [2, 384, 41472], P(None, ('grp', 'dev')), may hold values from -6 to 6
- derivatives: float32 [384, 512, 289], P(None, ('grp', 'dev')), may hold values from -0.6666667 to 0.6666667
Outputs:
- taylors: float32 [2, 384, 41472], P(None, ('grp', 'dev'))
The draws below stay inside these ranges and needn't reach their ends.
All inputs are finite; a program needn't handle non-finite values.
Results may differ from the reference program's by a relative error of at most 0.0001.
Values sent between devices are 32-bit elements; how exact they have to be, the bound alone decides.
A program may use at most 192 MiB of HBM per device.

```python
import math
import jax
import jax.numpy as jnp
import numpy as np
from jax import lax

ORDER = 8
COMP = 81
DCOMP = 289
NZ = 384
Q = 512


def block_levels(stream_key, shape, shards, low, largest):
    gain, own = 1.0, jax.random.fold_in(stream_key, 6)
    for position, shards_of in shards:
        draws = jnp.exp(jax.random.uniform(jax.random.fold_in(own, position), (shards_of,), jnp.float32, low / len(shards), largest / len(shards)))
        gain = gain * jnp.repeat(draws, shape[position] // shards_of).reshape([-1 if axis == position else 1 for axis in range(len(shape))])
    return gain


def bell_draw(key, shape, spread, most, pieces=(), kind=jnp.bfloat16):
    gain = block_levels(key, shape, pieces, -0.22, 0.18) if pieces else 1.0
    values = jax.random.normal(key, shape, jnp.float32) * spread * gain
    return jnp.minimum(jnp.maximum(values, -most), most).astype(kind)


def setup_inputs(seed: int = 0) -> dict:
    arg_keys = jax.random.split(jax.random.key(seed), 3)
    multipoles = bell_draw(arg_keys[0], (2, NZ, Q * COMP), 1.0, 6.0, ((1, 128),), jnp.float32)
    derivatives = bell_draw(arg_keys[1], (NZ, Q, DCOMP), (1.0 / (ORDER + 1)), 0.6666667, ((1, 128),), jnp.float32)
    return dict(multipoles=multipoles, derivatives=derivatives)


def reduced_terms(highest):
    listed = []
    for total in range(highest + 1):
        for upper in range(min(total, 1) + 1):
            for first in range(total - upper, -1, -1):
                listed.append((first, total - upper - first, upper))
    return listed

def coupling_tables(order):
    lower = reduced_terms(order)
    higher = reduced_terms(2 * order)
    where = {}
    for place, triple in enumerate(higher):
        where[triple] = place
    count = len(lower)
    first_index = np.zeros((count, count), np.int32)
    second_index = np.zeros((count, count), np.int32)
    first_sign = np.zeros((count, count), np.float32)
    second_sign = np.zeros((count, count), np.float32)
    for left, one in enumerate(lower):
        for right, other in enumerate(lower):
            summed = (one[0] + other[0], one[1] + other[1], one[2] + other[2])
            if summed[2] <= 1:
                first_index[left, right] = where[summed]
                first_sign[left, right] = 1.0
            else:
                first_index[left, right] = where[summed[0] + 2, summed[1], 0]
                second_index[left, right] = where[summed[0], summed[1] + 2, 0]
                first_sign[left, right] = -1.0
                second_sign[left, right] = -1.0
    return (first_index, second_index, first_sign, second_sign)

def dft_tables(length, positions):
    kvalues = jnp.arange(length, dtype=jnp.int32)
    phase = kvalues[:, None] * positions[None, :] % length
    angle = 2.0 * math.pi / length * phase.astype(jnp.float32)
    factor = 1.0 / math.sqrt(length)
    cosine = jnp.cos(angle) * factor
    sine = jnp.sin(angle) * factor
    forward = jnp.stack([jnp.stack([cosine, sine], 1), jnp.stack([-sine, cosine], 1)], 0)
    inverse = jnp.stack([jnp.stack([cosine.T, -sine.T], 1), jnp.stack([sine.T, cosine.T], 1)], 0)
    return (forward, inverse)

def contract_block(deriv_block, moment_block, tables):
    first_index, second_index, first_sign, second_sign = tables
    coupling = first_sign[:, :, None] * deriv_block[first_index] + second_sign[:, :, None] * deriv_block[second_index]
    return jnp.einsum('abp,bip->aip', coupling, moment_block, precision=lax.Precision.HIGHEST)

def contract_all(deriv, moment, order):
    tables = coupling_tables(order)
    total = deriv.shape[1]
    width = math.gcd(total, 768)
    count = total // width

    def step(index, result):
        start = (index * width).astype(jnp.int32)
        deriv_block = lax.dynamic_slice_in_dim(deriv, start, width, 1)
        moment_block = lax.dynamic_slice_in_dim(moment, start, width, 2)
        return lax.dynamic_update_slice_in_dim(result, contract_block(deriv_block, moment_block, tables), start, 2)
    return lax.fori_loop(0, count, step, jnp.zeros(moment.shape, moment.dtype))

def reference(multipoles, derivatives):
    modes = multipoles.reshape(2, NZ, Q, COMP)
    forward, inverse = dft_tables(NZ, jnp.arange(NZ, dtype=jnp.int32))
    spectrum = jnp.einsum('rkiz,izqc->crqk', forward, modes, precision=lax.Precision.HIGHEST)
    spectrum = spectrum.reshape(COMP, 2, Q * NZ)
    deriv_flat = jnp.transpose(derivatives, (2, 1, 0)).reshape(DCOMP, Q * NZ)
    taylor_k = contract_all(deriv_flat, spectrum, ORDER).reshape(COMP, 2, Q, NZ)
    result = jnp.einsum('rzik,ciqk->rzqc', inverse, taylor_k, precision=lax.Precision.HIGHEST)
    return result.reshape(2, NZ, Q * COMP)
```

```python
import functools
import math

import jax
import jax.numpy as jnp
import ml_dtypes
import numpy as np
from jax import lax
from jax.experimental import pallas as pl
from jax.experimental.pallas import tpu as pltpu
from jax.sharding import PartitionSpec as P

ORDER = 8
MESH = pl.DeviceIdType.MESH
F32 = jnp.float32
BF16 = jnp.bfloat16

COMP = 81
NDEV = 128
INNER = 64
NZ = 384
ZL = 3
COLS = 324
HALF = 162
REST = 34
ZROWS = 648
LEAD = 8
PLANE_ROWS = LEAD + ZL * ZROWS + 16
QS = 82
NX = 409


def reduced_terms(highest):
    listed = []
    for total in range(highest + 1):
        for upper in range(min(total, 1) + 1):
            for first in range(total - upper, -1, -1):
                listed.append((first, total - upper - first, upper))
    return listed


LOWER = {t: n for n, t in enumerate(reduced_terms(ORDER))}
HIGHER = {t: n for n, t in enumerate(reduced_terms(2 * ORDER))}


def extended_index():
    place, parts = {}, []
    for total in range(2 * ORDER - 1):
        for first in range(total, -1, -1):
            second = total - first
            place[first, second] = 289 + len(parts)
            parts.append((HIGHER[first + 2, second, 0], HIGHER[first, second + 2, 0]))
    return place, parts


SECOND, SECOND_PARTS = extended_index()


def deriv_place(i, j, c):
    return HIGHER[i, j, c] if c <= 1 else SECOND[i, j]


def dft_table():
    z = (3 * np.arange(NDEV)[None, :] + np.arange(ZL)[:, None]).reshape(-1)
    k = np.arange(NZ)
    angle = 2.0 * np.pi / NZ * (z[:, None] * k[None, :] % NZ)
    c, s = np.cos(angle) / math.sqrt(NZ), np.sin(angle) / math.sqrt(NZ)
    w = np.block([[c, -s], [s, c]])
    high = w.astype(ml_dtypes.bfloat16)
    low = (w - high.astype(np.float64)).astype(ml_dtypes.bfloat16)
    return high, low


def split(x):
    high = x.astype(BF16)
    return high, (x - high.astype(F32)).astype(BF16)


def iotas():
    lane = lax.broadcasted_iota(jnp.int32, (8, 128), 1)
    row = lax.broadcasted_iota(jnp.int32, (8, 128), 0)
    return lane, row


def column_start(owner, h):
    start = COLS * owner + HALF * h
    return start // 128, start % 128


def pack(plane, msg, h, d):
    lane, row = iotas()
    tile, off = column_start(d, h)
    here = lane >= off
    rel = jnp.where(here, lane - off, lane - off + 128)
    main = rest = None
    for z in range(ZL):
        at = LEAD + z * ZROWS + 2 * tile - 2 * z
        v = jnp.where(here, plane[pl.ds(at, 8), :], plane[pl.ds(at + 2, 8), :])
        main = v if z == 0 else jnp.where(row >= 2 * z, v, main)
        at = LEAD + z * ZROWS + 2 * tile - 4
        v = jnp.where(here, plane[pl.ds(at, 8), :], plane[pl.ds(at + 2, 8), :])
        if z:
            v = pltpu.roll(v, REST * z, 1)
        rest = v if z == 0 else jnp.where(rel >= REST * z, v, rest)
    msg[h, pl.ds(pl.multiple_of(8 * d, 8), 8), :] = jnp.where(row >= 6, rest, main)


def unpack(got, plane, h, s):
    lane, row = iotas()
    tile, off = column_start(s, h)
    here = lane >= off
    rel = jnp.where(here, lane - off, lane - off + 128)
    m = got[h, pl.ds(pl.multiple_of(8 * s, 8), 8), :]
    for z in range(ZL):
        mine = (row >= 2 * z) & (row < 2 * z + 2)
        at = LEAD + z * ZROWS + 2 * tile - 2 * z
        pltpu.store(plane.at[pl.ds(at, 8), :], m, mask=mine & here)
        pltpu.store(plane.at[pl.ds(at + 2, 8), :], m, mask=mine & ~here)
        v = pltpu.roll(m, 128 - REST * z, 1) if z else m
        mine = (row >= 6) & (rel < REST)
        at = LEAD + z * ZROWS + 2 * tile - 4
        pltpu.store(plane.at[pl.ds(at, 8), :], v, mask=mine & here)
        pltpu.store(plane.at[pl.ds(at + 2, 8), :], v, mask=mine & ~here)


def send_all(me, msg, got, send_sem, recv_sem, h):
    @pl.loop(1, NDEV)
    def _(i):
        d = (me + i) % NDEV
        pltpu.make_async_remote_copy(
            src_ref=msg.at[h, pl.ds(pl.multiple_of(8 * d, 8), 8), :],
            dst_ref=got.at[h, pl.ds(pl.multiple_of(8 * me, 8), 8), :],
            send_sem=send_sem.at[h],
            recv_sem=recv_sem.at[h],
            device_id=(d // INNER, d % INNER),
            device_id_type=MESH,
        ).start()


def own_copy(me, msg, got, sem, h):
    mine = pl.ds(pl.multiple_of(8 * me, 8), 8)
    return pltpu.make_async_copy(msg.at[h, mine, :], got.at[h, mine, :], sem.at[h])


def wait_bytes(buf, sem, h):
    part = buf.at[h, pl.ds(0, 8 * (NDEV - 1)), :]
    pltpu.make_async_copy(part, part, sem.at[h]).wait()


def prepare(deriv, table):
    @pl.loop(0, 289)
    def _(n):
        for kc in range(3):
            v = deriv[n, :, pl.ds(128 * kc, 128)]
            table[kc, n] = jnp.concatenate([v, v], axis=0)

    @pl.loop(0, 3)
    def _(kc):
        for n, (one, two) in enumerate(SECOND_PARTS):
            table[kc, 289 + n] = -(table[kc, one] + table[kc, two])


def gather_columns(got, xbuf, h, off):
    back = (128 - off) % 128
    base = 2 * h * QS
    for r in range(2):
        for z in range(ZL):
            v = got[h, pl.ds(2 * z + r, NDEV, stride=8), :]
            v = pltpu.roll(v, back, 1).T
            xbuf[r * ZL + z, base : base + 81, :] = v[:81]
            xbuf[r * ZL + z, base + QS : base + QS + 47, :] = v[81:]
        v = pltpu.roll(got[h, pl.ds(6 + r, NDEV, stride=8), :], back, 1).T
        for z in range(ZL):
            at = base + QS + 47
            xbuf[r * ZL + z, at : at + REST, :] = v[REST * z : REST * z + REST]


def forward(xbuf, whigh, wlow, sbuf):
    x = jnp.concatenate([xbuf[n] for n in range(6)], axis=1)
    high, low = split(x)
    dot = functools.partial(jnp.dot, preferred_element_type=F32)
    out = dot(high, whigh[...]) + dot(low, whigh[...]) + dot(high, wlow[...])
    for r in range(2):
        for kc in range(3):
            at = r * NZ + kc * 128
            sbuf[kc, r * 4 * QS : (r + 1) * 4 * QS, :] = out[:, at : at + 128]


def contract(table, sbuf, stage, tbuf):
    @pl.loop(0, 3)
    def _(kc):
        for b in range(COMP):
            stage[b] = sbuf[kc, pl.ds(b, 8, stride=QS), :]
        for c in range(2):
            for i in range(ORDER + 1 - c):
                rows = ORDER + 1 - c - i
                acc = [None] * rows
                for c2 in range(2):
                    for i2 in range(ORDER + 1 - c2):
                        terms = ORDER + 1 - c2 - i2
                        seen = {}
                        for j2 in range(terms):
                            s = stage[LOWER[i2, j2, c2]]
                            for j in range(rows):
                                if j + j2 not in seen:
                                    place = deriv_place(i + i2, j + j2, c + c2)
                                    seen[j + j2] = table[kc, place]
                                v = seen[j + j2] * s
                                acc[j] = v if acc[j] is None else acc[j] + v
                for j in range(rows):
                    tbuf[kc, pl.ds(LOWER[i, j, c], 8, stride=COMP), :] = acc[j]


def backward(tbuf, tarr, whigh, wlow, ybuf):
    for r in range(2):
        for kc in range(3):
            n, at = r * 3 + kc, r * COLS
            tarr[n, 0:128, :] = tbuf[kc, at : at + 128, :]
            tarr[n, 128:256, :] = tbuf[kc, at + HALF : at + HALF + 128, :]
            tarr[n, 256 : 256 + REST, :] = tbuf[kc, at + 128 : at + HALF, :]
            tarr[n, 256 + REST : 256 + 2 * REST, :] = tbuf[kc, at + HALF + 128 : at + COLS, :]
            tarr[n, 256 + 2 * REST :, :] = jnp.zeros((128 - 2 * REST, 128), F32)
    t = jnp.concatenate([tarr[n] for n in range(6)], axis=1)
    high, low = split(t)
    dims = (((1,), (1,)), ((), ()))
    dot = functools.partial(lax.dot_general, dimension_numbers=dims, preferred_element_type=F32)
    ybuf[...] = dot(whigh[...], high) + dot(whigh[...], low) + dot(wlow[...], high)


def scatter_columns(ybuf, msg, h, off):
    lane = lax.broadcasted_iota(jnp.int32, (NDEV, 128), 1)
    rel = jnp.where(lane >= off, lane - off, lane - off + 128)
    for r in range(2):
        rest = None
        for z in range(ZL):
            at = (r * ZL + z) * NDEV
            v = ybuf[at : at + NDEV, 128 * h : 128 * h + 128]
            msg[h, pl.ds(2 * z + r, NDEV, stride=8), :] = pltpu.roll(v, off, 1)
            shift = (off + REST * z + 128 - REST * h) % 128
            v = pltpu.roll(ybuf[at : at + NDEV, 256:384], shift, 1)
            rest = v if z == 0 else jnp.where(rel >= REST * z, v, rest)
        msg[h, pl.ds(6 + r, NDEV, stride=8), :] = rest


def kernel(
    planes_hbm, deriv_hbm, whigh_hbm, wlow_hbm, out_hbm,
    plane, outp, deriv, whigh, wlow, table, msg, got, msg2, got2, xbuf, sbuf, stage, tbuf, tarr, ybuf,
    load_sem, own_sem, send_sem, recv_sem, own_sem2, send_sem2, recv_sem2,
):
    me = lax.axis_index("grp") * INNER + lax.axis_index("dev")
    loads = [
        pltpu.make_async_copy(planes_hbm, plane.at[pl.ds(LEAD, ZL * ZROWS), :], load_sem.at[0]),
        pltpu.make_async_copy(deriv_hbm, deriv, load_sem.at[1]),
        pltpu.make_async_copy(whigh_hbm, whigh, load_sem.at[2]),
        pltpu.make_async_copy(wlow_hbm, wlow, load_sem.at[3]),
    ]
    for copy in loads:
        copy.start()
    barrier = pltpu.get_barrier_semaphore()

    @pl.loop(1, NDEV)
    def _(i):
        d = (me + i) % NDEV
        pl.semaphore_signal(barrier, inc=1, device_id=(d // INNER, d % INNER), device_id_type=MESH)

    plane[0:LEAD, :] = jnp.zeros((LEAD, 128), F32)
    plane[LEAD + ZL * ZROWS :, :] = jnp.zeros((16, 128), F32)
    loads[0].wait()
    for h in range(2):

        @pl.loop(0, NDEV, unroll=4)
        def _(d):
            pack(plane, msg, h, d)

    pl.semaphore_wait(barrier, NDEV - 1)
    for h in range(2):
        send_all(me, msg, got, send_sem, recv_sem, h)
        own_copy(me, msg, got, own_sem, h).start()
    for copy in loads[1:]:
        copy.wait()
    prepare(deriv, table)
    for h in range(2):
        own_copy(me, msg, got, own_sem, h).wait()
        wait_bytes(got, recv_sem, h)
        gather_columns(got, xbuf, h, column_start(me, h)[1])
    forward(xbuf, whigh, wlow, sbuf)
    contract(table, sbuf, stage, tbuf)
    backward(tbuf, tarr, whigh, wlow, ybuf)
    for h in range(2):
        scatter_columns(ybuf, msg2, h, column_start(me, h)[1])
        send_all(me, msg2, got2, send_sem2, recv_sem2, h)
        own_copy(me, msg2, got2, own_sem2, h).start()
    for h in range(2):
        own_copy(me, msg2, got2, own_sem2, h).wait()
        wait_bytes(got2, recv_sem2, h)

        @pl.loop(0, NDEV, unroll=4)
        def _(s):
            unpack(got2, outp, h, s)

    store = pltpu.make_async_copy(outp.at[pl.ds(LEAD, ZL * ZROWS), :], out_hbm, load_sem.at[0])
    store.start()
    for h in range(2):
        wait_bytes(msg, send_sem, h)
        wait_bytes(msg2, send_sem2, h)
    store.wait()


def on_device(multipoles, derivatives):
    planes = jnp.transpose(multipoles, (1, 0, 2)).reshape(ZL, 2, COLS, 128)
    planes = jnp.transpose(planes, (0, 2, 1, 3)).reshape(ZL * ZROWS, 128)
    deriv = jnp.transpose(derivatives, (2, 1, 0))
    high, low = dft_table()
    vmem, dma = pltpu.VMEM, pltpu.SemaphoreType.DMA
    out = pl.pallas_call(
        kernel,
        out_shape=jax.ShapeDtypeStruct((ZL * ZROWS, 128), F32),
        in_specs=[pl.BlockSpec(memory_space=pl.ANY)] * 4,
        out_specs=pl.BlockSpec(memory_space=pl.ANY),
        scratch_shapes=[
            vmem((PLANE_ROWS, 128), F32),
            vmem((PLANE_ROWS, 128), F32),
            vmem((289, 4, NZ), F32),
            vmem((2 * NZ, 2 * NZ), BF16),
            vmem((2 * NZ, 2 * NZ), BF16),
            vmem((3, NX, 8, 128), F32),
            vmem((2, 8 * NDEV, 128), F32),
            vmem((2, 8 * NDEV, 128), F32),
            vmem((2, 8 * NDEV, 128), F32),
            vmem((2, 8 * NDEV, 128), F32),
            vmem((6, 4 * QS, 128), F32),
            vmem((3, 8 * QS, 128), F32),
            vmem((COMP, 8, 128), F32),
            vmem((3, 8 * COMP, 128), F32),
            vmem((6, 384, 128), F32),
            vmem((2 * NZ, 384), F32),
            dma((4,)), dma((2,)), dma((2,)), dma((2,)), dma((2,)), dma((2,)), dma((2,)),
        ],
        compiler_params=pltpu.CompilerParams(
            collective_id=0, has_side_effects=True, vmem_limit_bytes=60 * 1024 * 1024
        ),
        name="m2l",
    )(planes, deriv, jnp.asarray(high), jnp.asarray(low))
    out = jnp.transpose(out.reshape(ZL, COLS, 2, 128), (0, 2, 1, 3)).reshape(ZL, 2, COLS * 128)
    return jnp.transpose(out, (1, 0, 2))


def solution(mesh):
    in_specs = (P(None, ("grp", "dev"), None), P(None, ("grp", "dev"), None))
    out_specs = P(None, ("grp", "dev"), None)
    return jax.shard_map(
        on_device, mesh=mesh, in_specs=in_specs, out_specs=out_specs, check_vma=False
    )
```

```python
import functools
import math

import jax
import jax.numpy as jnp
import ml_dtypes
import numpy as np
from jax import lax
from jax.experimental import pallas as pl
from jax.experimental.layout import Layout, with_layout_constraint
from jax.experimental.pallas import tpu as pltpu
from jax.sharding import PartitionSpec as P

ORDER = 8
MESH = pl.DeviceIdType.MESH
F32 = jnp.float32
BF16 = jnp.bfloat16

COMP = 81
NDEV = 128
INNER = 64
NZ = 384
ZL = 3
COLS = 324
HALF = 162
REST = 34
ZROWS = 648
LEAD = 8
PLANE_ROWS = LEAD + ZL * ZROWS + 16
QS = 82
MROWS = 168


def reduced_terms(highest):
    listed = []
    for total in range(highest + 1):
        for upper in range(min(total, 1) + 1):
            for first in range(total - upper, -1, -1):
                listed.append((first, total - upper - first, upper))
    return listed


LOWER = {t: n for n, t in enumerate(reduced_terms(ORDER))}
HIGHER = {t: n for n, t in enumerate(reduced_terms(2 * ORDER))}


class Plan:
    def __init__(self):
        self.count = len(HIGHER)
        self.second, self.level1, self.level2 = [], [], []
        self.pairs = []
        self.one = {}
        top = 2 * ORDER
        for total in range(top + 1):
            for i in range(total + 1):
                j = total - i
                d0, d1 = HIGHER[i, j, 0], HIGHER.get((i, j, 1))
                self.one["p", i, j] = d1
                self.one["a", i, j] = d0
                if d1 is not None:
                    self.one["a", i, j] = self.fresh()
                    self.level1.append((self.one["a", i, j], d0, d1))
                self.one["b", i, j] = None
                if total <= top - 2:
                    self.one["b", i, j] = self.fresh()
                    self.second.append((self.one["b", i, j], HIGHER[i + 2, j, 0], HIGHER[i, j + 2, 0], d1))
        for total in range(top + 1):
            for i in range(total + 1):
                for kind in "pab":
                    own, other = self.one[kind, i, total - i], self.one.get((kind, i + 1, total - i))
                    if own is not None:
                        self.pairs.append((own, other))
        self.two = {}
        for kind in "pab":
            for i in range(top + 1):
                for m in range(ORDER + 1):
                    even, odd, after = (self.one.get((kind, i, 2 * m + e)) for e in range(3))
                    self.two[kind, "p", i, m] = odd
                    self.two[kind, "a", i, m] = self.minus(even, odd)
                    self.two[kind, "b", i, m] = self.minus(after, odd)

    def fresh(self):
        self.count += 1
        return self.count - 1

    def minus(self, x, y):
        if y is None:
            return x
        slot = self.fresh()
        self.level2.append((slot, x, y))
        return slot


PLAN = Plan()


def dft_table():
    z = (3 * np.arange(NDEV)[None, :] + np.arange(ZL)[:, None]).reshape(-1)
    k = np.arange(NZ)
    angle = 2.0 * np.pi / NZ * (z[:, None] * k[None, :] % NZ)
    c, s = np.cos(angle) / math.sqrt(NZ), np.sin(angle) / math.sqrt(NZ)
    w = np.block([[c, -s], [s, c]])
    high = w.astype(ml_dtypes.bfloat16)
    low = (w - high.astype(np.float64)).astype(ml_dtypes.bfloat16)
    return high, low


def split(x):
    high = x.astype(BF16)
    return high, (x - high.astype(F32)).astype(BF16)


def iotas():
    lane = lax.broadcasted_iota(jnp.int32, (8, 128), 1)
    row = lax.broadcasted_iota(jnp.int32, (8, 128), 0)
    return lane, row


def column_start(owner, h):
    start = COLS * owner + HALF * h
    return start // 128, start % 128


def pack(plane, msg, h, d):
    lane, row = iotas()
    tile, off = column_start(d, h)
    here = lane >= off
    rel = jnp.where(here, lane - off, lane - off + 128)
    main = rest = None
    for z in range(ZL):
        at = LEAD + z * ZROWS + 2 * tile - 2 * z
        v = jnp.where(here, plane[pl.ds(at, 8), :], plane[pl.ds(at + 2, 8), :])
        main = v if z == 0 else jnp.where(row >= 2 * z, v, main)
        at = LEAD + z * ZROWS + 2 * tile - 4
        v = jnp.where(here, plane[pl.ds(at, 8), :], plane[pl.ds(at + 2, 8), :])
        if z:
            v = pltpu.roll(v, REST * z, 1)
        rest = v if z == 0 else jnp.where(rel >= REST * z, v, rest)
    msg[h, pl.ds(pl.multiple_of(8 * d, 8), 8), :] = jnp.where(row >= 6, rest, main)


def unpack(got, plane, h, s):
    lane, row = iotas()
    tile, off = column_start(s, h)
    here = lane >= off
    rel = jnp.where(here, lane - off, lane - off + 128)
    m = got[h, pl.ds(pl.multiple_of(8 * s, 8), 8), :]
    for z in range(ZL):
        mine = (row >= 2 * z) & (row < 2 * z + 2)
        at = LEAD + z * ZROWS + 2 * tile - 2 * z
        pltpu.store(plane.at[pl.ds(at, 8), :], m, mask=mine & here)
        pltpu.store(plane.at[pl.ds(at + 2, 8), :], m, mask=mine & ~here)
        v = pltpu.roll(m, 128 - REST * z, 1) if z else m
        mine = (row >= 6) & (rel < REST)
        at = LEAD + z * ZROWS + 2 * tile - 4
        pltpu.store(plane.at[pl.ds(at, 8), :], v, mask=mine & here)
        pltpu.store(plane.at[pl.ds(at + 2, 8), :], v, mask=mine & ~here)


def send_all(me, msg, got, send_sem, recv_sem, h):
    @pl.loop(1, NDEV)
    def _(i):
        d = (me + i) % NDEV
        pltpu.make_async_remote_copy(
            src_ref=msg.at[h, pl.ds(pl.multiple_of(8 * d, 8), 8), :],
            dst_ref=got.at[h, pl.ds(pl.multiple_of(8 * me, 8), 8), :],
            send_sem=send_sem.at[h],
            recv_sem=recv_sem.at[h],
            device_id=(d // INNER, d % INNER),
            device_id_type=MESH,
        ).start()


def own_copy(me, msg, got, sem, h):
    mine = pl.ds(pl.multiple_of(8 * me, 8), 8)
    return pltpu.make_async_copy(msg.at[h, mine, :], got.at[h, mine, :], sem.at[h])


def wait_bytes(buf, sem, h):
    part = buf.at[h, pl.ds(0, 8 * (NDEV - 1)), :]
    pltpu.make_async_copy(part, part, sem.at[h]).wait()


def prepare_base(deriv, table):
    @pl.loop(0, len(HIGHER))
    def _(n):
        v = [deriv[n, :, pl.ds(128 * kc, 128)] for kc in range(3)]
        for h in range(2):
            v0, v1, v2 = (x[2 * h : 2 * h + 2] for x in v)
            table[h, n] = jnp.concatenate([v0, v0, v1, v1], axis=0)
            table[2 + h, n] = jnp.concatenate([v2, v2, v2, v2], axis=0)


def prepare_tables(table):
    row = lax.broadcasted_iota(jnp.int32, (8, 128), 0)

    @pl.loop(0, 4)
    def _(n):
        for slot, x, y in PLAN.level1:
            table[n, slot] = table[n, x] - table[n, y]
        for slot, x, y, z in PLAN.second:
            table[n, slot] = -(table[n, x] + table[n, y]) - table[n, z]

    @pl.loop(2, 4)
    def _(n):
        for own, other in PLAN.pairs:
            up = jnp.zeros((8, 128), F32) if other is None else table[n, other]
            table[n, own] = jnp.where(row < 4, table[n, own], up)

    @pl.loop(0, 4)
    def _(n):
        for slot, x, y in PLAN.level2:
            table[n, slot] = -table[n, y] if x is None else table[n, x] - table[n, y]


def gather_columns(got, xbuf, h, off):
    back = (128 - off) % 128
    for r in range(2):
        for z in range(ZL):
            v = got[h, pl.ds(2 * z + r, NDEV, stride=8), :]
            v = pltpu.roll(v, back, 1).T
            xbuf[r * ZL + z, 0:81, :] = v[:81]
            xbuf[r * ZL + z, QS : QS + 47, :] = v[81:]
        v = pltpu.roll(got[h, pl.ds(6 + r, NDEV, stride=8), :], back, 1).T
        for z in range(ZL):
            xbuf[r * ZL + z, QS + 47 : QS + 47 + REST, :] = v[REST * z : REST * z + REST]


def forward(xbuf, whigh, wlow, sbuf):
    x = jnp.concatenate([xbuf[n] for n in range(6)], axis=1)
    high, low = split(x)
    dot = functools.partial(jnp.dot, preferred_element_type=F32)
    out = dot(high, whigh[...]) + dot(low, whigh[...]) + dot(high, wlow[...])
    for r in range(2):
        for kc in range(3):
            at, row = r * NZ + kc * 128, (2 * kc + r) * 2 * QS
            sbuf[row : row + 2 * QS, :] = out[: 2 * QS, at : at + 128]


def contract(table, n, stage, paired, finish):
    step = 2 if paired else 1
    inputs = {}
    spare = [COMP]

    def added(x, y):
        if y is None:
            return x
        stage[spare[0]] = stage[x] + stage[y]
        spare[0] += 1
        return spare[0] - 1

    part = [{}, {}]
    for c in range(2):
        for i in range(0, ORDER + 1 - c, step):
            for j in range(ORDER + 1 - c - i):
                part[c][i, j] = LOWER[i, j, c]
    inputs["a"], inputs["b"] = part
    inputs["p"] = {x: added(s, part[1].get(x)) for x, s in part[0].items()}
    leaves = {}
    for kind in "pab":
        even = {(i, j // 2): s for (i, j), s in inputs[kind].items() if j % 2 == 0}
        odd = {(i, j // 2): s for (i, j), s in inputs[kind].items() if j % 2 == 1}
        leaves[kind] = {"a": even, "b": odd, "p": {x: added(s, odd.get(x)) for x, s in even.items()}}

    def leaf_row(kind, sub, i, rows):
        acc = [None] * rows
        seen = {}
        for (i2, m2), slot in leaves[kind][sub].items():
            s = stage[slot]
            for m in range(rows):
                key = i + i2, m + m2
                place = PLAN.two.get((kind, sub, *key))
                if place is None:
                    continue
                if key not in seen:
                    seen[key] = table[n, place]
                v = seen[key] * s
                acc[m] = v if acc[m] is None else acc[m] + v
        return acc

    def row_of(kind, i, count):
        evens, odds = (count + 1) // 2, count // 2
        p = leaf_row(kind, "p", i, evens)
        a = leaf_row(kind, "a", i, evens)
        b = leaf_row(kind, "b", i, odds) if odds else []
        out = [None] * count
        for m in range(evens):
            out[2 * m] = a[m] if p[m] is None else p[m] + a[m]
        for m in range(odds):
            out[2 * m + 1] = p[m] + b[m]
        return out

    for i in range(ORDER + 1):
        count = ORDER + 1 - i
        p = row_of("p", i, count)
        a = row_of("a", i, count)
        b = row_of("b", i, count - 1) if count > 1 else []
        for j in range(count):
            finish(LOWER[i, j, 0], a[j] if p[j] is None else p[j] + a[j])
        for j in range(count - 1):
            finish(LOWER[i, j, 1], p[j] + b[j])


def contract_half(table, h, sbuf, stage, stage2, tbuf):
    row = lax.broadcasted_iota(jnp.int32, (8, 128), 0)
    for b in range(COMP):
        stage[b] = sbuf[pl.ds(b, 8, stride=QS), :]
    for (i, j, c), b in LOWER.items():
        if i % 2 == 0:
            v = sbuf[pl.ds(8 * QS + b, 8, stride=QS), :]
            up = LOWER.get((i + 1, j, c))
            up = jnp.zeros((8, 128), F32) if up is None else sbuf[pl.ds(4 * QS + up, 8, stride=QS), :]
            stage2[b] = jnp.where(row < 4, v, up)

    def finish(a, v):
        tbuf[pl.ds(a, 8, stride=COMP), :] = v

    def finish2(a, v):
        tbuf[pl.ds(8 * COMP + a, 8, stride=COMP), :] = v + pltpu.roll(v, 4, 0)

    contract(table, h, stage, False, finish)
    contract(table, 2 + h, stage2, True, finish2)


def backward(tbuf, vhigh, vlow, ybuf):
    t = jnp.concatenate([tbuf[HALF * (2 * kc + r) : HALF * (2 * kc + r) + MROWS, :] for r in range(2) for kc in range(3)], axis=1)
    high, low = split(t)
    dot = functools.partial(jnp.dot, preferred_element_type=F32)
    ybuf[...] = dot(high, vhigh[...]) + dot(low, vhigh[...]) + dot(high, vlow[...])


def scatter_columns(ybuf, rest, msg, h, off):
    for r in range(2):
        for z in range(ZL):
            at = (r * ZL + z) * NDEV
            v = ybuf[0:128, at : at + NDEV].T
            msg[h, pl.ds(2 * z + r, NDEV, stride=8), :] = pltpu.roll(v, off, 1)
            rest[r, REST * z : REST * z + REST, :] = ybuf[128:HALF, at : at + NDEV]
        v = pltpu.roll(rest[r].T, off, 1)
        msg[h, pl.ds(6 + r, NDEV, stride=8), :] = v


def transpose_table(w, v):
    for x in range(6):
        for y in range(6):
            block = w[128 * x : 128 * x + 128, 128 * y : 128 * y + 128].astype(F32)
            v[128 * y : 128 * y + 128, 128 * x : 128 * x + 128] = block.T.astype(BF16)


def kernel(
    planes_hbm, deriv_hbm, whigh_hbm, wlow_hbm, out_hbm,
    plane, outp, deriv, whigh, wlow, vhigh, vlow, table, msg, got, msg2, got2, xbuf, sbuf, stage, stage2, tbuf, ybuf, rest,
    load_sem, own_sem, send_sem, recv_sem, own_sem2, send_sem2, recv_sem2,
):
    me = lax.axis_index("grp") * INNER + lax.axis_index("dev")
    loads = [
        pltpu.make_async_copy(planes_hbm, plane.at[pl.ds(LEAD, ZL * ZROWS), :], load_sem.at[0]),
        pltpu.make_async_copy(deriv_hbm, deriv, load_sem.at[1]),
        pltpu.make_async_copy(whigh_hbm, whigh, load_sem.at[2]),
        pltpu.make_async_copy(wlow_hbm, wlow, load_sem.at[3]),
    ]
    for copy in loads:
        copy.start()
    barrier = pltpu.get_barrier_semaphore()

    @pl.loop(1, NDEV)
    def _(i):
        d = (me + i) % NDEV
        pl.semaphore_signal(barrier, inc=1, device_id=(d // INNER, d % INNER), device_id_type=MESH)

    plane[0:LEAD, :] = jnp.zeros((LEAD, 128), F32)
    plane[LEAD + ZL * ZROWS :, :] = jnp.zeros((16, 128), F32)
    loads[0].wait()

    for h in range(2):

        @pl.loop(0, NDEV, unroll=4)
        def _(d):
            pack(plane, msg, h, d)

        if h == 0:
            pl.semaphore_wait(barrier, NDEV - 1)
        send_all(me, msg, got, send_sem, recv_sem, h)
        own_copy(me, msg, got, own_sem, h).start()
    for copy in loads[1:]:
        copy.wait()
    prepare_base(deriv, table)
    prepare_tables(table)
    transpose_table(whigh, vhigh)
    transpose_table(wlow, vlow)
    xbuf[:, 2 * QS :, :] = jnp.zeros((6, MROWS - 2 * QS, 128), F32)
    rest[:, 3 * REST :, :] = jnp.zeros((2, 128 - 3 * REST, 128), F32)

    @pl.loop(0, 2)
    def _(h):
        off = column_start(me, h)[1]
        own_copy(me, msg, got, own_sem, h).wait()
        wait_bytes(got, recv_sem, h)
        gather_columns(got, xbuf, h, off)
        forward(xbuf, whigh, wlow, sbuf)
        contract_half(table, h, sbuf, stage, stage2, tbuf)
        backward(tbuf, vhigh, vlow, ybuf)
        scatter_columns(ybuf, rest, msg2, h, off)
        send_all(me, msg2, got2, send_sem2, recv_sem2, h)
        own_copy(me, msg2, got2, own_sem2, h).start()

    for h in range(2):
        own_copy(me, msg2, got2, own_sem2, h).wait()
        wait_bytes(got2, recv_sem2, h)

        @pl.loop(0, NDEV, unroll=4)
        def _(s):
            unpack(got2, outp, h, s)

    store = pltpu.make_async_copy(outp.at[pl.ds(LEAD, ZL * ZROWS), :], out_hbm, load_sem.at[0])
    store.start()
    for h in range(2):
        wait_bytes(msg, send_sem, h)
        wait_bytes(msg2, send_sem2, h)
    store.wait()


def on_device(multipoles, derivatives):
    planes = with_layout_constraint(multipoles.reshape(2, ZL, COLS, 128), Layout((1, 2, 0, 3)))
    planes = jnp.transpose(planes, (1, 2, 0, 3)).reshape(ZL * ZROWS, 128)
    deriv = jnp.transpose(derivatives, (2, 1, 0))
    high, low = dft_table()
    vmem, dma = pltpu.VMEM, pltpu.SemaphoreType.DMA
    out = pl.pallas_call(
        kernel,
        out_shape=jax.ShapeDtypeStruct((ZL * ZROWS, 128), F32),
        in_specs=[pl.BlockSpec(memory_space=pl.ANY)] * 4,
        out_specs=pl.BlockSpec(memory_space=pl.ANY),
        scratch_shapes=[
            vmem((PLANE_ROWS, 128), F32),
            vmem((PLANE_ROWS, 128), F32),
            vmem((289, 4, NZ), F32),
            vmem((2 * NZ, 2 * NZ), BF16),
            vmem((2 * NZ, 2 * NZ), BF16),
            vmem((2 * NZ, 2 * NZ), BF16),
            vmem((2 * NZ, 2 * NZ), BF16),
            vmem((4, PLAN.count, 8, 128), F32),
            vmem((2, 8 * NDEV, 128), F32),
            vmem((2, 8 * NDEV, 128), F32),
            vmem((2, 8 * NDEV, 128), F32),
            vmem((2, 8 * NDEV, 128), F32),
            vmem((6, MROWS, 128), F32),
            vmem((16 * QS, 128), F32),
            vmem((3 * COMP, 8, 128), F32),
            vmem((3 * COMP, 8, 128), F32),
            vmem((16 * COMP, 128), F32),
            vmem((MROWS, 2 * NZ), F32),
            vmem((2, 128, 128), F32),
            dma((4,)), dma((2,)), dma((2,)), dma((2,)), dma((2,)), dma((2,)), dma((2,)),
        ],
        compiler_params=pltpu.CompilerParams(
            collective_id=0, has_side_effects=True, vmem_limit_bytes=60 * 1024 * 1024
        ),
        name="m2l",
    )(planes, deriv, jnp.asarray(high), jnp.asarray(low))
    out = jnp.transpose(out.reshape(ZL, COLS, 2, 128), (0, 2, 1, 3)).reshape(ZL, 2, COLS * 128)
    return jnp.transpose(out, (1, 0, 2))


def solution(mesh):
    in_specs = (P(None, ("grp", "dev"), None), P(None, ("grp", "dev"), None))
    out_specs = P(None, ("grp", "dev"), None)
    return jax.shard_map(
        on_device, mesh=mesh, in_specs=in_specs, out_specs=out_specs, check_vma=False
    )
```

```python
import functools
import math

import jax
import jax.numpy as jnp
import ml_dtypes
import numpy as np
from jax import lax
from jax.experimental import pallas as pl
from jax.experimental.layout import Layout, with_layout_constraint
from jax.experimental.pallas import tpu as pltpu
from jax.sharding import PartitionSpec as P

ORDER = 8
MESH = pl.DeviceIdType.MESH
F32 = jnp.float32
BF16 = jnp.bfloat16

COMP = 81
NDEV = 128
INNER = 64
NZ = 384
ZL = 3
COLS = 324
HALF = 162
REST = 34
ZROWS = 648
LEAD = 8
PLANE_ROWS = LEAD + ZL * ZROWS + 16


def reduced_terms(highest):
    listed = []
    for total in range(highest + 1):
        for upper in range(min(total, 1) + 1):
            for first in range(total - upper, -1, -1):
                listed.append((first, total - upper - first, upper))
    return listed


LOWER = {t: n for n, t in enumerate(reduced_terms(ORDER))}
HIGHER = {t: n for n, t in enumerate(reduced_terms(2 * ORDER))}


class Plan:
    def __init__(self):
        self.count = len(HIGHER)
        self.second, self.level1, self.level2 = [], [], []
        self.pairs = []
        self.one = {}
        top = 2 * ORDER
        for total in range(top + 1):
            for i in range(total + 1):
                j = total - i
                d0, d1 = HIGHER[i, j, 0], HIGHER.get((i, j, 1))
                self.one["p", i, j] = d1
                self.one["a", i, j] = d0
                if d1 is not None:
                    self.one["a", i, j] = self.fresh()
                    self.level1.append((self.one["a", i, j], d0, d1))
                self.one["b", i, j] = None
                if total <= top - 2:
                    self.one["b", i, j] = self.fresh()
                    self.second.append((self.one["b", i, j], HIGHER[i + 2, j, 0], HIGHER[i, j + 2, 0], d1))
        for total in range(top + 1):
            for i in range(total + 1):
                for kind in "pab":
                    own, other = self.one[kind, i, total - i], self.one.get((kind, i + 1, total - i))
                    if own is not None:
                        self.pairs.append((own, other))
        self.two = {}
        for kind in "pab":
            for i in range(top + 1):
                for m in range(ORDER + 1):
                    even, odd, after = (self.one.get((kind, i, 2 * m + e)) for e in range(3))
                    self.two[kind, "p", i, m] = odd
                    self.two[kind, "a", i, m] = self.minus(even, odd)
                    self.two[kind, "b", i, m] = self.minus(after, odd)

    def fresh(self):
        self.count += 1
        return self.count - 1

    def minus(self, x, y):
        if y is None:
            return x
        slot = self.fresh()
        self.level2.append((slot, x, y))
        return slot


PLAN = Plan()


def dft_table():
    z = (3 * np.arange(NDEV)[None, :] + np.arange(ZL)[:, None]).reshape(-1)
    k = np.arange(NZ)
    angle = 2.0 * np.pi / NZ * (z[:, None] * k[None, :] % NZ)
    c, s = np.cos(angle) / math.sqrt(NZ), np.sin(angle) / math.sqrt(NZ)
    w = np.block([[c, -s], [s, c]])
    high = w.astype(ml_dtypes.bfloat16)
    low = (w - high.astype(np.float64)).astype(ml_dtypes.bfloat16)
    return high, low


def split(x):
    high = x.astype(BF16)
    return high, (x - high.astype(F32)).astype(BF16)


def iotas():
    lane = lax.broadcasted_iota(jnp.int32, (8, 128), 1)
    row = lax.broadcasted_iota(jnp.int32, (8, 128), 0)
    return lane, row


def column_start(owner, h):
    start = COLS * owner + HALF * h
    return start >> 7, start & 127


def pack(plane, msg, h, d):
    lane, row = iotas()
    tile, off = column_start(d, h)
    here = lane >= off
    rel = jnp.where(here, lane - off, lane - off + 128)
    main = rest = None
    for z in range(ZL):
        at = LEAD + z * ZROWS + 2 * tile - 2 * z
        v = jnp.where(here, plane[pl.ds(at, 8), :], plane[pl.ds(at + 2, 8), :])
        main = v if z == 0 else jnp.where(row >= 2 * z, v, main)
        at = LEAD + z * ZROWS + 2 * tile - 4
        v = jnp.where(here, plane[pl.ds(at, 8), :], plane[pl.ds(at + 2, 8), :])
        if z:
            v = pltpu.roll(v, REST * z, 1)
        rest = v if z == 0 else jnp.where(rel >= REST * z, v, rest)
    msg[h, pl.ds(pl.multiple_of(8 * d, 8), 8), :] = jnp.where(row >= 6, rest, main)


def unpack(got, plane, h, s):
    lane, row = iotas()
    tile, off = column_start(s, h)
    here = lane >= off
    column = (row >> 1) * 128 + lane - off
    mask = (column >= 0) & (column < HALF)
    first, second = row < 2, row < 4
    m = got[h, pl.ds(pl.multiple_of(8 * s, 8), 8), :]
    down, up, up2 = pltpu.roll(m, 2, 0), pltpu.roll(m, 6, 0), pltpu.roll(m, 4, 0)
    for z, (top, mid) in enumerate(((m, down), (up, m), (up2, up))):
        rest, rest2 = up2, up
        if z:
            rest, rest2 = pltpu.roll(up2, 128 - REST * z, 1), pltpu.roll(up, 128 - REST * z, 1)
        v = jnp.where(first, top, jnp.where(second, jnp.where(here, rest, mid), rest2))
        pltpu.store(plane.at[pl.ds(LEAD + z * ZROWS + 2 * tile, 8), :], v, mask=mask)


def each_other(me, action):
    step = 9

    @pl.loop(0, (NDEV - 2) // step)
    def _(t):
        for u in range(step):
            action((me + step * t + u + 1) & (NDEV - 1))

    action((me + NDEV - 1) & (NDEV - 1))


def device(d):
    return (d >> 6, d & (INNER - 1))


def send_all(me, msg, got, send_sem, recv_sem, h):
    def send(d):
        pltpu.make_async_remote_copy(
            src_ref=msg.at[h, pl.ds(pl.multiple_of(8 * d, 8), 8), :],
            dst_ref=got.at[h, pl.ds(pl.multiple_of(8 * me, 8), 8), :],
            send_sem=send_sem.at[h],
            recv_sem=recv_sem.at[h],
            device_id=device(d),
            device_id_type=MESH,
        ).start()

    each_other(me, send)


def own_copy(me, msg, got, sem, h):
    mine = pl.ds(pl.multiple_of(8 * me, 8), 8)
    return pltpu.make_async_copy(msg.at[h, mine, :], got.at[h, mine, :], sem.at[h])


def wait_bytes(buf, sem, h):
    part = buf.at[h, pl.ds(0, 8 * (NDEV - 1)), :]
    pltpu.make_async_copy(part, part, sem.at[h]).wait()


def prepare_base(deriv, table):
    @pl.loop(0, 17)
    def _(t):
        for u in range(17):
            n = 17 * t + u
            v = [deriv[n, :, pl.ds(128 * kc, 128)] for kc in range(3)]
            for h in range(2):
                v0, v1, v2 = (x[2 * h : 2 * h + 2] for x in v)
                table[h, n] = jnp.concatenate([v0, v0, v1, v1], axis=0)
                table[2 + h, n] = jnp.concatenate([v2, v2, v2, v2], axis=0)


def prepare_tables(table):
    row = lax.broadcasted_iota(jnp.int32, (8, 128), 0)

    @pl.loop(0, 4)
    def _(n):
        for slot, x, y in PLAN.level1:
            table[n, slot] = table[n, x] - table[n, y]
        for slot, x, y, z in PLAN.second:
            table[n, slot] = -(table[n, x] + table[n, y]) - table[n, z]

    @pl.loop(2, 4)
    def _(n):
        for own, other in PLAN.pairs:
            up = jnp.zeros((8, 128), F32) if other is None else table[n, other]
            table[n, own] = jnp.where(row < 4, table[n, own], up)

    @pl.loop(0, 4)
    def _(n):
        for slot, x, y in PLAN.level2:
            table[n, slot] = -table[n, y] if x is None else table[n, x] - table[n, y]


def put(high, low, n, v, lanes):
    h, l = split(v)
    high[128 * n : 128 * n + 128, lanes] = h
    low[128 * n : 128 * n + 128, lanes] = l


def gather_columns(got, xhigh, xlow, h, off):
    for r in range(2):
        rest = got[h, pl.ds(6 + r, NDEV, stride=8), :]
        for z in range(ZL):
            v = got[h, pl.ds(2 * z + r, NDEV, stride=8), :]
            put(xhigh, xlow, r * ZL + z, pltpu.roll(v, (128 - off) & 127, 1), slice(0, 128))
            v = pltpu.roll(rest, (256 - off - REST * z) & 127, 1)
            put(xhigh, xlow, r * ZL + z, v, slice(128, 256))


def product(whigh, wlow, high, low):
    dot = functools.partial(jnp.dot, preferred_element_type=F32)
    return dot(whigh[...], high[...]) + dot(whigh[...], low[...]) + dot(wlow[...], high[...])


def forward(xhigh, xlow, vhigh, vlow, sbuf):
    out = product(vhigh, vlow, xhigh, xlow)
    for r in range(2):
        for kc in range(3):
            at, row = 128 * (3 * r + kc), (2 * kc + r) * HALF
            sbuf[row : row + 128, :] = out[at : at + 128, 0:128].T
            sbuf[row + 128 : row + HALF, :] = out[at : at + 128, 128:256].T[:REST]


def contract(table, n, stage, paired, finish):
    step = 2 if paired else 1
    inputs = {}
    spare = [COMP]

    def added(x, y):
        if y is None:
            return x
        stage[spare[0]] = stage[x] + stage[y]
        spare[0] += 1
        return spare[0] - 1

    part = [{}, {}]
    for c in range(2):
        for i in range(0, ORDER + 1 - c, step):
            for j in range(ORDER + 1 - c - i):
                part[c][i, j] = LOWER[i, j, c]
    inputs["a"], inputs["b"] = part
    inputs["p"] = {x: added(s, part[1].get(x)) for x, s in part[0].items()}
    leaves = {}
    for kind in "pab":
        even = {(i, j // 2): s for (i, j), s in inputs[kind].items() if j % 2 == 0}
        odd = {(i, j // 2): s for (i, j), s in inputs[kind].items() if j % 2 == 1}
        leaves[kind] = {"a": even, "b": odd, "p": {x: added(s, odd.get(x)) for x, s in even.items()}}

    def leaf_rows(kind, sub, counts):
        acc = {i: [None] * count for i, count in counts.items()}
        mine = {}
        for (i2, m2), slot in leaves[kind][sub].items():
            mine.setdefault(i2, []).append((m2, slot))
        loaded = {}
        for top in sorted({i + i2 for i in counts for i2 in mine}):
            seen = {}
            for i, count in counts.items():
                for m2, slot in mine.get(top - i, ()):
                    for m in range(count):
                        place = PLAN.two.get((kind, sub, top, m + m2))
                        if place is None:
                            continue
                        if slot not in loaded:
                            loaded[slot] = stage[slot]
                        if m + m2 not in seen:
                            seen[m + m2] = table[n, place]
                        v = seen[m + m2] * loaded[slot]
                        acc[i][m] = v if acc[i][m] is None else acc[i][m] + v
        return acc

    def rows_of(kind, counts):
        evens, odds = ({i: (count + e) // 2 for i, count in counts.items()} for e in (1, 0))
        p = leaf_rows(kind, "p", evens)
        a = leaf_rows(kind, "a", evens)
        b = leaf_rows(kind, "b", odds)
        out = {i: [None] * count for i, count in counts.items()}
        for i in counts:
            for m in range(evens[i]):
                out[i][2 * m] = a[i][m] if p[i][m] is None else p[i][m] + a[i][m]
            for m in range(odds[i]):
                out[i][2 * m + 1] = p[i][m] + b[i][m]
        return out

    left = list(range(ORDER + 1))
    while left:
        group = [i for i in (left[0], left[0] + step) if i in left]
        left = [i for i in left if i not in group]
        counts = {i: ORDER + 1 - i for i in group}
        p = rows_of("p", counts)
        a = rows_of("a", counts)
        for i in group:
            for j in range(counts[i]):
                finish(LOWER[i, j, 0], a[i][j] if p[i][j] is None else p[i][j] + a[i][j])
        b = rows_of("b", {i: count - 1 for i, count in counts.items()})
        for i in group:
            for j in range(counts[i] - 1):
                finish(LOWER[i, j, 1], p[i][j] + b[i][j])


def contract_half(table, h, sbuf, stage, stage2, tbuf):
    row = lax.broadcasted_iota(jnp.int32, (8, 128), 0)
    for b in range(COMP):
        stage[b] = sbuf[pl.ds(b, 8, stride=COMP), :]
    for (i, j, c), b in LOWER.items():
        if i % 2 == 0:
            v = sbuf[pl.ds(8 * COMP + b, 8, stride=COMP), :]
            up = LOWER.get((i + 1, j, c))
            up = jnp.zeros((8, 128), F32) if up is None else sbuf[pl.ds(4 * COMP + up, 8, stride=COMP), :]
            stage2[b] = jnp.where(row < 4, v, up)

    def finish(a, v):
        tbuf[pl.ds(a, 8, stride=COMP), :] = v

    def finish2(a, v):
        tbuf[pl.ds(8 * COMP + a, 8, stride=COMP), :] = v + pltpu.roll(v, 4, 0)

    contract(table, h, stage, False, finish)
    contract(table, 2 + h, stage2, True, finish2)


def backward(tbuf, whigh, wlow, thigh, tlow, ybuf):
    for r in range(2):
        for kc in range(3):
            row = (2 * kc + r) * HALF
            put(thigh, tlow, 3 * r + kc, tbuf[row : row + 128, :].T, slice(0, 128))
            put(thigh, tlow, 3 * r + kc, tbuf[row + 128 : row + 256, :].T, slice(128, 256))
    ybuf[...] = product(whigh, wlow, thigh, tlow)


def scatter_columns(ybuf, msg, h, off):
    lane = lax.broadcasted_iota(jnp.int32, (NDEV, 128), 1)
    rel = jnp.where(lane >= off, lane - off, lane - off + 128)
    for r in range(2):
        rest = None
        for z in range(ZL):
            at = (r * ZL + z) * NDEV
            msg[h, pl.ds(2 * z + r, NDEV, stride=8), :] = pltpu.roll(ybuf[at : at + NDEV, 0:128], off, 1)
            v = pltpu.roll(ybuf[at : at + NDEV, 128:256], (off + REST * z) & 127, 1)
            rest = v if z == 0 else jnp.where(rel >= REST * z, v, rest)
        msg[h, pl.ds(6 + r, NDEV, stride=8), :] = rest


def transpose_table(w, v):
    for x in range(6):
        for y in range(6):
            block = w[128 * x : 128 * x + 128, 128 * y : 128 * y + 128].astype(F32)
            v[128 * y : 128 * y + 128, 128 * x : 128 * x + 128] = block.T.astype(BF16)


def kernel(
    planes_hbm, deriv_hbm, whigh_hbm, wlow_hbm, out_hbm,
    plane, outp, deriv, whigh, wlow, vhigh, vlow, table, msg, got, msg2, got2, xhigh, xlow, sbuf, stage, stage2, tbuf, ybuf,
    load_sem, own_sem, send_sem, recv_sem, own_sem2, send_sem2, recv_sem2,
):
    me = lax.axis_index("grp") * INNER + lax.axis_index("dev")
    loads = [
        pltpu.make_async_copy(planes_hbm, plane.at[pl.ds(LEAD, ZL * ZROWS), :], load_sem.at[0]),
        pltpu.make_async_copy(deriv_hbm, deriv, load_sem.at[1]),
        pltpu.make_async_copy(whigh_hbm, whigh, load_sem.at[2]),
        pltpu.make_async_copy(wlow_hbm, wlow, load_sem.at[3]),
    ]
    for copy in loads:
        copy.start()
    barrier = pltpu.get_barrier_semaphore()

    each_other(me, lambda d: pl.semaphore_signal(barrier, inc=1, device_id=device(d), device_id_type=MESH))
    plane[0:LEAD, :] = jnp.zeros((LEAD, 128), F32)
    plane[LEAD + ZL * ZROWS :, :] = jnp.zeros((16, 128), F32)
    loads[0].wait()

    for h in range(2):

        @pl.loop(0, NDEV, unroll=8)
        def _(d):
            pack(plane, msg, h, d)

    pl.semaphore_wait(barrier, NDEV - 1)
    for h in range(2):
        send_all(me, msg, got, send_sem, recv_sem, h)
        own_copy(me, msg, got, own_sem, h).start()
    for copy in loads[1:]:
        copy.wait()
    prepare_base(deriv, table)
    prepare_tables(table)
    transpose_table(whigh, vhigh)
    transpose_table(wlow, vlow)
    @pl.loop(0, 2)
    def _(h):
        off = column_start(me, h)[1]
        own_copy(me, msg, got, own_sem, h).wait()
        wait_bytes(got, recv_sem, h)
        gather_columns(got, xhigh, xlow, h, off)
        forward(xhigh, xlow, vhigh, vlow, sbuf)
        contract_half(table, h, sbuf, stage, stage2, tbuf)
        backward(tbuf, whigh, wlow, xhigh, xlow, ybuf)
        scatter_columns(ybuf, msg2, h, off)
        send_all(me, msg2, got2, send_sem2, recv_sem2, h)
        own_copy(me, msg2, got2, own_sem2, h).start()

    for h in range(2):
        own_copy(me, msg2, got2, own_sem2, h).wait()
        wait_bytes(got2, recv_sem2, h)

        @pl.loop(0, NDEV, unroll=8)
        def _(s):
            unpack(got2, outp, h, s)

    store = pltpu.make_async_copy(outp.at[pl.ds(LEAD, ZL * ZROWS), :], out_hbm, load_sem.at[0])
    store.start()
    for h in range(2):
        wait_bytes(msg, send_sem, h)
        wait_bytes(msg2, send_sem2, h)
    store.wait()


def on_device(multipoles, derivatives):
    planes = with_layout_constraint(multipoles.reshape(2, ZL, COLS, 128), Layout((1, 2, 0, 3)))
    planes = jnp.transpose(planes, (1, 2, 0, 3)).reshape(ZL * ZROWS, 128)
    deriv = jnp.transpose(derivatives, (2, 1, 0))
    high, low = dft_table()
    vmem, dma = pltpu.VMEM, pltpu.SemaphoreType.DMA
    out = pl.pallas_call(
        kernel,
        out_shape=jax.ShapeDtypeStruct((ZL * ZROWS, 128), F32),
        in_specs=[pl.BlockSpec(memory_space=pl.ANY)] * 4,
        out_specs=pl.BlockSpec(memory_space=pl.ANY),
        scratch_shapes=[
            vmem((PLANE_ROWS, 128), F32),
            vmem((PLANE_ROWS, 128), F32),
            vmem((289, 4, NZ), F32),
            vmem((2 * NZ, 2 * NZ), BF16),
            vmem((2 * NZ, 2 * NZ), BF16),
            vmem((2 * NZ, 2 * NZ), BF16),
            vmem((2 * NZ, 2 * NZ), BF16),
            vmem((4, PLAN.count, 8, 128), F32),
            vmem((2, 8 * NDEV, 128), F32),
            vmem((2, 8 * NDEV, 128), F32),
            vmem((2, 8 * NDEV, 128), F32),
            vmem((2, 8 * NDEV, 128), F32),
            vmem((2 * NZ, 256), BF16),
            vmem((2 * NZ, 256), BF16),
            vmem((16 * COMP, 128), F32),
            vmem((3 * COMP, 8, 128), F32),
            vmem((3 * COMP, 8, 128), F32),
            vmem((16 * COMP, 128), F32),
            vmem((2 * NZ, 256), F32),
            dma((4,)), dma((2,)), dma((2,)), dma((2,)), dma((2,)), dma((2,)), dma((2,)),
        ],
        compiler_params=pltpu.CompilerParams(
            collective_id=0, has_side_effects=True, vmem_limit_bytes=60 * 1024 * 1024
        ),
        name="m2l",
    )(planes, deriv, jnp.asarray(high), jnp.asarray(low))
    out = jnp.transpose(out.reshape(ZL, COLS, 2, 128), (0, 2, 1, 3)).reshape(ZL, 2, COLS * 128)
    return jnp.transpose(out, (1, 0, 2))


def solution(mesh):
    in_specs = (P(None, ("grp", "dev"), None), P(None, ("grp", "dev"), None))
    out_specs = P(None, ("grp", "dev"), None)
    return jax.shard_map(
        on_device, mesh=mesh, in_specs=in_specs, out_specs=out_specs, check_vma=False
    )
```

```python
import functools
import math

import jax
import jax.numpy as jnp
import ml_dtypes
import numpy as np
from jax import lax
from jax.experimental import pallas as pl
from jax.experimental.layout import Layout, with_layout_constraint
from jax.experimental.pallas import tpu as pltpu
from jax.sharding import PartitionSpec as P

ORDER = 8
MESH = pl.DeviceIdType.MESH
F32 = jnp.float32
BF16 = jnp.bfloat16

COMP = 81
NDEV = 128
INNER = 64
NZ = 384
ZL = 3
COLS = 324
HALF = 162
REST = 34
ZROWS = 648
LEAD = 8
OUT_ROWS = ZL * ZROWS + 8
PLANE_ROWS = LEAD + ZL * ZROWS + 16


def reduced_terms(highest):
    listed = []
    for total in range(highest + 1):
        for upper in range(min(total, 1) + 1):
            for first in range(total - upper, -1, -1):
                listed.append((first, total - upper - first, upper))
    return listed


LOWER = {t: n for n, t in enumerate(reduced_terms(ORDER))}
HIGHER = {t: n for n, t in enumerate(reduced_terms(2 * ORDER))}


class Plan:
    def __init__(self):
        self.count = len(HIGHER)
        self.second, self.level1, self.level2 = [], [], []
        self.pairs = []
        self.one = {}
        top = 2 * ORDER
        for total in range(top + 1):
            for i in range(total + 1):
                j = total - i
                d0, d1 = HIGHER[i, j, 0], HIGHER.get((i, j, 1))
                self.one["p", i, j] = d1
                self.one["a", i, j] = d0
                if d1 is not None:
                    self.one["a", i, j] = self.fresh()
                    self.level1.append((self.one["a", i, j], d0, d1))
                self.one["b", i, j] = None
                if total <= top - 2:
                    self.one["b", i, j] = self.fresh()
                    self.second.append((self.one["b", i, j], HIGHER[i + 2, j, 0], HIGHER[i, j + 2, 0], d1))
        for total in range(top + 1):
            for i in range(total + 1):
                for kind in "pab":
                    own, other = self.one[kind, i, total - i], self.one.get((kind, i + 1, total - i))
                    if own is not None:
                        self.pairs.append((own, other))
        self.two = {}
        for kind in "pab":
            for i in range(top + 1):
                for m in range(ORDER + 1):
                    even, odd, after = (self.one.get((kind, i, 2 * m + e)) for e in range(3))
                    self.two[kind, "p", i, m] = odd
                    self.two[kind, "a", i, m] = self.minus(even, odd)
                    self.two[kind, "b", i, m] = self.minus(after, odd)

    def fresh(self):
        self.count += 1
        return self.count - 1

    def minus(self, x, y):
        if y is None:
            return x
        slot = self.fresh()
        self.level2.append((slot, x, y))
        return slot


PLAN = Plan()


def dft_table():
    z = (3 * np.arange(NDEV)[None, :] + np.arange(ZL)[:, None]).reshape(-1)
    k = np.arange(NZ)
    angle = 2.0 * np.pi / NZ * (z[:, None] * k[None, :] % NZ)
    c, s = np.cos(angle) / math.sqrt(NZ), np.sin(angle) / math.sqrt(NZ)
    w = np.block([[c, -s], [s, c]])
    high = w.astype(ml_dtypes.bfloat16)
    low = (w - high.astype(np.float64)).astype(ml_dtypes.bfloat16)
    return high, low


def split(x):
    high = x.astype(BF16)
    return high, (x - high.astype(F32)).astype(BF16)


def iotas():
    lane = lax.broadcasted_iota(jnp.int32, (8, 128), 1)
    row = lax.broadcasted_iota(jnp.int32, (8, 128), 0)
    return lane, row


def column_start(owner, h):
    start = COLS * owner + HALF * h
    return start >> 7, start & 127


def pack(plane, msg, h, d):
    lane, row = iotas()
    tile, off = column_start(d, h)
    here = lane >= off
    rel = jnp.where(here, lane - off, lane - off + 128)
    main = rest = None
    for z in range(ZL):
        at = LEAD + z * ZROWS + 2 * tile - 2 * z
        v = jnp.where(here, plane[pl.ds(at, 8), :], plane[pl.ds(at + 2, 8), :])
        main = v if z == 0 else jnp.where(row >= 2 * z, v, main)
        at = LEAD + z * ZROWS + 2 * tile - 4
        v = jnp.where(here, plane[pl.ds(at, 8), :], plane[pl.ds(at + 2, 8), :])
        if z:
            v = pltpu.roll(v, REST * z, 1)
        rest = v if z == 0 else jnp.where(rel >= REST * z, v, rest)
    msg[h, pl.ds(pl.multiple_of(8 * d, 8), 8), :] = jnp.where(row >= 6, rest, main)


def unpack(got, plane, h, s):
    lane, row = iotas()
    tile, off = column_start(s, h)
    here = lane >= off
    column = (row >> 1) * 128 + lane - off
    mask = (column >= 0) & (column < HALF)
    first, second = row < 2, row < 4
    m = got[h, pl.ds(pl.multiple_of(8 * s, 8), 8), :]
    down, up, up2 = pltpu.roll(m, 2, 0), pltpu.roll(m, 6, 0), pltpu.roll(m, 4, 0)
    for z, (top, mid) in enumerate(((m, down), (up, m), (up2, up))):
        rest, rest2 = up2, up
        if z:
            rest, rest2 = pltpu.roll(up2, 128 - REST * z, 1), pltpu.roll(up, 128 - REST * z, 1)
        v = jnp.where(first, top, jnp.where(second, jnp.where(here, rest, mid), rest2))
        pltpu.store(plane.at[pl.ds(z * ZROWS + 2 * tile, 8), :], v, mask=mask)


def each_other(me, action):
    step = 9

    @pl.loop(0, (NDEV - 2) // step)
    def _(t):
        for u in range(step):
            action((me + step * t + u + 1) & (NDEV - 1))

    action((me + NDEV - 1) & (NDEV - 1))


def device(d):
    return (d >> 6, d & (INNER - 1))


def send_all(me, msg, got, send_sem, recv_sem, h):
    def send(d):
        pltpu.make_async_remote_copy(
            src_ref=msg.at[h, pl.ds(pl.multiple_of(8 * d, 8), 8), :],
            dst_ref=got.at[h, pl.ds(pl.multiple_of(8 * me, 8), 8), :],
            send_sem=send_sem.at[h],
            recv_sem=recv_sem.at[h],
            device_id=device(d),
            device_id_type=MESH,
        ).start()

    each_other(me, send)


def own_copy(me, msg, got, sem, h):
    mine = pl.ds(pl.multiple_of(8 * me, 8), 8)
    return pltpu.make_async_copy(msg.at[h, mine, :], got.at[h, mine, :], sem.at[h])


def wait_bytes(buf, sem, h):
    part = buf.at[h, pl.ds(0, 8 * (NDEV - 1)), :]
    pltpu.make_async_copy(part, part, sem.at[h]).wait()


def prepare_base(deriv, table):
    @pl.loop(0, 17)
    def _(t):
        for u in range(17):
            n = 17 * t + u
            v = [deriv[n, :, pl.ds(128 * kc, 128)] for kc in range(3)]
            for h in range(2):
                v0, v1, v2 = (x[2 * h : 2 * h + 2] for x in v)
                table[h, n] = jnp.concatenate([v0, v0, v1, v1], axis=0)
                table[2 + h, n] = jnp.concatenate([v2, v2, v2, v2], axis=0)


def prepare_tables(table):
    row = lax.broadcasted_iota(jnp.int32, (8, 128), 0)

    @pl.loop(0, 4)
    def _(n):
        for slot, x, y in PLAN.level1:
            table[n, slot] = table[n, x] - table[n, y]
        for slot, x, y, z in PLAN.second:
            table[n, slot] = -(table[n, x] + table[n, y]) - table[n, z]

    @pl.loop(2, 4)
    def _(n):
        for own, other in PLAN.pairs:
            up = jnp.zeros((8, 128), F32) if other is None else table[n, other]
            table[n, own] = jnp.where(row < 4, table[n, own], up)

    @pl.loop(0, 4)
    def _(n):
        for slot, x, y in PLAN.level2:
            table[n, slot] = -table[n, y] if x is None else table[n, x] - table[n, y]


def put(high, low, n, v, lanes):
    h, l = split(v)
    high[128 * n : 128 * n + 128, lanes] = h
    low[128 * n : 128 * n + 128, lanes] = l


def gather_columns(got, xhigh, xlow, h, off):
    for r in range(2):
        rest = got[h, pl.ds(6 + r, NDEV, stride=8), :]
        for z in range(ZL):
            v = got[h, pl.ds(2 * z + r, NDEV, stride=8), :]
            put(xhigh, xlow, r * ZL + z, pltpu.roll(v, (128 - off) & 127, 1), slice(0, 128))
            v = pltpu.roll(rest, (256 - off - REST * z) & 127, 1)
            put(xhigh, xlow, r * ZL + z, v, slice(128, 256))


def product(whigh, wlow, high, low):
    dot = functools.partial(jnp.dot, preferred_element_type=F32)
    return dot(whigh[...], high[...]) + dot(whigh[...], low[...]) + dot(wlow[...], high[...])


def forward(xhigh, xlow, vhigh, vlow, sbuf):
    out = product(vhigh, vlow, xhigh, xlow)
    for r in range(2):
        for kc in range(3):
            at, row = 128 * (3 * r + kc), (2 * kc + r) * HALF
            sbuf[row : row + 128, :] = out[at : at + 128, 0:128].T
            sbuf[row + 128 : row + HALF, :] = out[at : at + 128, 128:256].T[:REST]


def contract(table, n, stage, paired, finish, hold, gate):
    step = 2 if paired else 1
    inputs = {}
    spare = [COMP]

    def added(x, y):
        if y is None:
            return x
        stage[spare[0]] = stage[x] + stage[y]
        spare[0] += 1
        return spare[0] - 1

    part = [{}, {}]
    for c in range(2):
        for i in range(0, ORDER + 1 - c, step):
            for j in range(ORDER + 1 - c - i):
                part[c][i, j] = LOWER[i, j, c]
    inputs["a"], inputs["b"] = part
    inputs["p"] = {x: added(s, part[1].get(x)) for x, s in part[0].items()}
    leaves = {}
    for kind in "pab":
        even = {(i, j // 2): s for (i, j), s in inputs[kind].items() if j % 2 == 0}
        odd = {(i, j // 2): s for (i, j), s in inputs[kind].items() if j % 2 == 1}
        leaves[kind] = {"a": even, "b": odd, "p": {x: added(s, odd.get(x)) for x, s in even.items()}}

    def leaf_rows(kind, sub, counts):
        acc = {i: [None] * count for i, count in counts.items()}
        mine = {}
        for (i2, m2), slot in leaves[kind][sub].items():
            mine.setdefault(i2, []).append((m2, slot))
        loaded = {}
        for top in sorted({i + i2 for i in counts for i2 in mine}):
            seen = {}
            for i, count in counts.items():
                for m2, slot in mine.get(top - i, ()):
                    for m in range(count):
                        place = PLAN.two.get((kind, sub, top, m + m2))
                        if place is None:
                            continue
                        if slot not in loaded:
                            loaded[slot] = stage[slot]
                        if m + m2 not in seen:
                            seen[m + m2] = table[n, place]
                        v = seen[m + m2] * loaded[slot]
                        acc[i][m] = v if acc[i][m] is None else acc[i][m] + v
        return acc

    def rows_of(kind, counts):
        evens, odds = ({i: (count + e) // 2 for i, count in counts.items()} for e in (1, 0))
        p = leaf_rows(kind, "p", evens)
        a = leaf_rows(kind, "a", evens)
        b = leaf_rows(kind, "b", odds)
        out = {i: [None] * count for i, count in counts.items()}
        for i in counts:
            for m in range(evens[i]):
                out[i][2 * m] = a[i][m] if p[i][m] is None else p[i][m] + a[i][m]
            for m in range(odds[i]):
                out[i][2 * m + 1] = p[i][m] + b[i][m]
        return out

    left = list(range(ORDER + 1))
    while left:
        group = [i for i in (left[0], left[0] + step) if i in left]
        left = [i for i in left if i not in group]
        counts = {i: ORDER + 1 - i for i in group}
        place = {}
        for i in group:
            for j in range(counts[i]):
                place[i, j] = len(place)
        known = set()

        @pl.when(gate)
        def _():
            p = rows_of("p", counts)
            for (i, j), at in place.items():
                if p[i][j] is not None:
                    hold[at] = p[i][j]
                    known.add((i, j))

        @pl.when(gate)
        def _():
            a = rows_of("a", counts)
            for (i, j), at in place.items():
                finish(LOWER[i, j, 0], hold[at] + a[i][j] if (i, j) in known else a[i][j])

        @pl.when(gate)
        def _():
            b = rows_of("b", {i: count - 1 for i, count in counts.items()})
            for i in group:
                for j in range(counts[i] - 1):
                    finish(LOWER[i, j, 1], hold[place[i, j]] + b[i][j])


def contract_half(table, h, sbuf, stage, stage2, tbuf, hold, gate):
    row = lax.broadcasted_iota(jnp.int32, (8, 128), 0)
    for b in range(COMP):
        stage[b] = sbuf[pl.ds(b, 8, stride=COMP), :]
    for (i, j, c), b in LOWER.items():
        if i % 2 == 0:
            v = sbuf[pl.ds(8 * COMP + b, 8, stride=COMP), :]
            up = LOWER.get((i + 1, j, c))
            up = jnp.zeros((8, 128), F32) if up is None else sbuf[pl.ds(4 * COMP + up, 8, stride=COMP), :]
            stage2[b] = jnp.where(row < 4, v, up)

    def finish(a, v):
        tbuf[pl.ds(a, 8, stride=COMP), :] = v

    def finish2(a, v):
        tbuf[pl.ds(8 * COMP + a, 8, stride=COMP), :] = v + pltpu.roll(v, 4, 0)

    contract(table, h, stage, False, finish, hold, gate)
    contract(table, 2 + h, stage2, True, finish2, hold, gate)


def backward(tbuf, whigh, wlow, thigh, tlow, ybuf):
    for r in range(2):
        for kc in range(3):
            row = (2 * kc + r) * HALF
            put(thigh, tlow, 3 * r + kc, tbuf[row : row + 128, :].T, slice(0, 128))
            put(thigh, tlow, 3 * r + kc, tbuf[row + 128 : row + 256, :].T, slice(128, 256))
    ybuf[...] = product(whigh, wlow, thigh, tlow)


def scatter_columns(ybuf, msg, h, off):
    lane = lax.broadcasted_iota(jnp.int32, (NDEV, 128), 1)
    rel = jnp.where(lane >= off, lane - off, lane - off + 128)
    for r in range(2):
        rest = None
        for z in range(ZL):
            at = (r * ZL + z) * NDEV
            msg[h, pl.ds(2 * z + r, NDEV, stride=8), :] = pltpu.roll(ybuf[at : at + NDEV, 0:128], off, 1)
            v = pltpu.roll(ybuf[at : at + NDEV, 128:256], (off + REST * z) & 127, 1)
            rest = v if z == 0 else jnp.where(rel >= REST * z, v, rest)
        msg[h, pl.ds(6 + r, NDEV, stride=8), :] = rest


def transpose_table(w, v):
    for x in range(6):
        for y in range(6):
            block = w[128 * x : 128 * x + 128, 128 * y : 128 * y + 128].astype(F32)
            v[128 * y : 128 * y + 128, 128 * x : 128 * x + 128] = block.T.astype(BF16)


def kernel(
    planes_hbm, deriv_hbm, whigh_hbm, wlow_hbm, out,
    plane, deriv, whigh, wlow, vhigh, vlow, table, msg, got, msg2, got2, xhigh, xlow, sbuf, stage, stage2, tbuf, hold, ybuf,
    load_sem, own_sem, send_sem, recv_sem, own_sem2, send_sem2, recv_sem2,
):
    me = lax.axis_index("grp") * INNER + lax.axis_index("dev")
    loads = [
        pltpu.make_async_copy(planes_hbm, plane.at[pl.ds(LEAD, ZL * ZROWS), :], load_sem.at[0]),
        pltpu.make_async_copy(deriv_hbm, deriv, load_sem.at[1]),
        pltpu.make_async_copy(whigh_hbm, whigh, load_sem.at[2]),
        pltpu.make_async_copy(wlow_hbm, wlow, load_sem.at[3]),
    ]
    for copy in loads:
        copy.start()
    barrier = pltpu.get_barrier_semaphore()

    each_other(me, lambda d: pl.semaphore_signal(barrier, inc=1, device_id=device(d), device_id_type=MESH))
    plane[0:LEAD, :] = jnp.zeros((LEAD, 128), F32)
    plane[LEAD + ZL * ZROWS :, :] = jnp.zeros((16, 128), F32)
    loads[0].wait()

    for h in range(2):

        @pl.loop(0, NDEV, unroll=8)
        def _(d):
            pack(plane, msg, h, d)

    pl.semaphore_wait(barrier, NDEV - 1)
    for h in range(2):
        send_all(me, msg, got, send_sem, recv_sem, h)
        own_copy(me, msg, got, own_sem, h).start()
    for copy in loads[1:]:
        copy.wait()
    prepare_base(deriv, table)
    prepare_tables(table)
    transpose_table(whigh, vhigh)
    transpose_table(wlow, vlow)
    @pl.loop(0, 2)
    def _(h):
        off = column_start(me, h)[1]
        own_copy(me, msg, got, own_sem, h).wait()
        wait_bytes(got, recv_sem, h)
        gather_columns(got, xhigh, xlow, h, off)
        forward(xhigh, xlow, vhigh, vlow, sbuf)
        contract_half(table, h, sbuf, stage, stage2, tbuf, hold, me >= 0)
        backward(tbuf, whigh, wlow, xhigh, xlow, ybuf)
        scatter_columns(ybuf, msg2, h, off)
        send_all(me, msg2, got2, send_sem2, recv_sem2, h)
        own_copy(me, msg2, got2, own_sem2, h).start()

    for h in range(2):
        own_copy(me, msg2, got2, own_sem2, h).wait()
        wait_bytes(got2, recv_sem2, h)

        @pl.loop(0, NDEV, unroll=8)
        def _(s):
            unpack(got2, out, h, s)

    for h in range(2):
        wait_bytes(msg, send_sem, h)
        wait_bytes(msg2, send_sem2, h)


def on_device(multipoles, derivatives):
    planes = with_layout_constraint(multipoles.reshape(2, ZL, COLS, 128), Layout((1, 2, 0, 3)))
    planes = jnp.transpose(planes, (1, 2, 0, 3)).reshape(ZL * ZROWS, 128)
    deriv = jnp.transpose(derivatives, (2, 1, 0))
    high, low = dft_table()
    vmem, dma = pltpu.VMEM, pltpu.SemaphoreType.DMA
    out = pl.pallas_call(
        kernel,
        out_shape=jax.ShapeDtypeStruct((OUT_ROWS, 128), F32),
        in_specs=[pl.BlockSpec(memory_space=pl.ANY)] * 4,
        out_specs=pl.BlockSpec(memory_space=pltpu.VMEM),
        scratch_shapes=[
            vmem((PLANE_ROWS, 128), F32),
            vmem((289, 4, NZ), F32),
            vmem((2 * NZ, 2 * NZ), BF16),
            vmem((2 * NZ, 2 * NZ), BF16),
            vmem((2 * NZ, 2 * NZ), BF16),
            vmem((2 * NZ, 2 * NZ), BF16),
            vmem((4, PLAN.count, 8, 128), F32),
            vmem((2, 8 * NDEV, 128), F32),
            vmem((2, 8 * NDEV, 128), F32),
            vmem((2, 8 * NDEV, 128), F32),
            vmem((2, 8 * NDEV, 128), F32),
            vmem((2 * NZ, 256), BF16),
            vmem((2 * NZ, 256), BF16),
            vmem((16 * COMP, 128), F32),
            vmem((3 * COMP, 8, 128), F32),
            vmem((3 * COMP, 8, 128), F32),
            vmem((16 * COMP, 128), F32),
            vmem((24, 8, 128), F32),
            vmem((2 * NZ, 256), F32),
            dma((4,)), dma((2,)), dma((2,)), dma((2,)), dma((2,)), dma((2,)), dma((2,)),
        ],
        compiler_params=pltpu.CompilerParams(
            collective_id=0, has_side_effects=True, vmem_limit_bytes=54000000
        ),
        name="m2l",
    )(planes, deriv, jnp.asarray(high), jnp.asarray(low))
    out = jnp.transpose(out[: ZL * ZROWS].reshape(ZL, COLS, 2, 128), (0, 2, 1, 3)).reshape(ZL, 2, COLS * 128)
    return jnp.transpose(out, (1, 0, 2))


def solution(mesh):
    in_specs = (P(None, ("grp", "dev"), None), P(None, ("grp", "dev"), None))
    out_specs = P(None, ("grp", "dev"), None)
    return jax.shard_map(
        on_device, mesh=mesh, in_specs=in_specs, out_specs=out_specs, check_vma=False
    )
```

```python
import functools
import math

import jax
import jax.numpy as jnp
import ml_dtypes
import numpy as np
from jax import lax
from jax.experimental import pallas as pl
from jax.experimental.layout import Layout, with_layout_constraint
from jax.experimental.pallas import tpu as pltpu
from jax.sharding import PartitionSpec as P

ORDER = 8
MESH = pl.DeviceIdType.MESH
F32 = jnp.float32
BF16 = jnp.bfloat16

COMP = 81
NDEV = 128
INNER = 64
NZ = 384
ZL = 3
COLS = 324
HALF = 162
REST = 34
MROWS = 168
ROOT = math.sqrt(3.0) / 2
ZROWS = 648
LEAD = 8
OUT_ROWS = ZL * ZROWS + 8
PLANE_ROWS = LEAD + ZL * ZROWS + 16


def reduced_terms(highest):
    listed = []
    for total in range(highest + 1):
        for upper in range(min(total, 1) + 1):
            for first in range(total - upper, -1, -1):
                listed.append((first, total - upper - first, upper))
    return listed


LOWER = {t: n for n, t in enumerate(reduced_terms(ORDER))}
HIGHER = {t: n for n, t in enumerate(reduced_terms(2 * ORDER))}


class Plan:
    def __init__(self):
        self.count = len(HIGHER)
        self.second, self.level1, self.level2 = [], [], []
        self.pairs = []
        self.one = {}
        top = 2 * ORDER
        for total in range(top + 1):
            for i in range(total + 1):
                j = total - i
                d0, d1 = HIGHER[i, j, 0], HIGHER.get((i, j, 1))
                self.one["p", i, j] = d1
                self.one["a", i, j] = d0
                if d1 is not None:
                    self.one["a", i, j] = self.fresh()
                    self.level1.append((self.one["a", i, j], d0, d1))
                self.one["b", i, j] = None
                if total <= top - 2:
                    self.one["b", i, j] = self.fresh()
                    self.second.append((self.one["b", i, j], HIGHER[i + 2, j, 0], HIGHER[i, j + 2, 0], d1))
        for total in range(top + 1):
            for i in range(total + 1):
                for kind in "pab":
                    own, other = self.one[kind, i, total - i], self.one.get((kind, i + 1, total - i))
                    if own is not None:
                        self.pairs.append((own, other))
        self.two = {}
        for kind in "pab":
            for i in range(top + 1):
                for m in range(ORDER + 1):
                    even, odd, after = (self.one.get((kind, i, 2 * m + e)) for e in range(3))
                    self.two[kind, "p", i, m] = odd
                    self.two[kind, "a", i, m] = self.minus(even, odd)
                    self.two[kind, "b", i, m] = self.minus(after, odd)

    def fresh(self):
        self.count += 1
        return self.count - 1

    def minus(self, x, y):
        if y is None:
            return x
        slot = self.fresh()
        self.level2.append((slot, x, y))
        return slot


PLAN = Plan()


def dft_tables():
    n = np.arange(NDEV)
    angle = 2.0 * np.pi / NDEV * (n[:, None] * n[None, :] % NDEV)
    c, s = np.cos(angle) / math.sqrt(NZ), np.sin(angle) / math.sqrt(NZ)
    out = []
    for w in (np.block([[c, -s], [s, c]]), np.block([[c, s], [-s, c]])):
        high = w.astype(ml_dtypes.bfloat16)
        out += [high, (w - high.astype(np.float64)).astype(ml_dtypes.bfloat16)]
    rows = np.concatenate(out + turn_rows())
    return np.pad(rows, ((0, 5120 - len(rows)), (0, 0)))


def turn_rows():
    angle = 2.0 * np.pi / NZ * np.arange(NDEV)
    left = np.zeros((16, 256))
    left[:4, :NDEV] = [f(z * angle) for z in (1, 2) for f in (np.cos, np.sin)]
    out = []
    for _ in range(3):
        out.append(left.astype(ml_dtypes.bfloat16))
        left = left - out[-1].astype(np.float64)
    return out


def split(x):
    high = x.astype(BF16)
    return high, (x - high.astype(F32)).astype(BF16)


def iotas():
    lane = lax.broadcasted_iota(jnp.int32, (8, 128), 1)
    row = lax.broadcasted_iota(jnp.int32, (8, 128), 0)
    return lane, row


def column_start(owner, h):
    start = COLS * owner + HALF * h
    return start >> 7, start & 127


def pack(plane, msg, h, d):
    lane, row = iotas()
    tile, off = column_start(d, h)
    here = lane >= off
    rel = jnp.where(here, lane - off, lane - off + 128)
    main = rest = None
    for z in range(ZL):
        at = LEAD + z * ZROWS + 2 * tile - 2 * z
        v = jnp.where(here, plane[pl.ds(at, 8), :], plane[pl.ds(at + 2, 8), :])
        main = v if z == 0 else jnp.where(row >= 2 * z, v, main)
        at = LEAD + z * ZROWS + 2 * tile - 4
        v = jnp.where(here, plane[pl.ds(at, 8), :], plane[pl.ds(at + 2, 8), :])
        if z:
            v = pltpu.roll(v, REST * z, 1)
        rest = v if z == 0 else jnp.where(rel >= REST * z, v, rest)
    msg[h, pl.ds(pl.multiple_of(8 * d, 8), 8), :] = jnp.where(row >= 6, rest, main)


def unpack(got, plane, h, s):
    lane, row = iotas()
    tile, off = column_start(s, h)
    here = lane >= off
    column = (row >> 1) * 128 + lane - off
    mask = (column >= 0) & (column < HALF)
    first, second = row < 2, row < 4
    m = got[h, pl.ds(pl.multiple_of(8 * s, 8), 8), :]
    down, up, up2 = pltpu.roll(m, 2, 0), pltpu.roll(m, 6, 0), pltpu.roll(m, 4, 0)
    for z, (top, mid) in enumerate(((m, down), (up, m), (up2, up))):
        rest, rest2 = up2, up
        if z:
            rest, rest2 = pltpu.roll(up2, 128 - REST * z, 1), pltpu.roll(up, 128 - REST * z, 1)
        v = jnp.where(first, top, jnp.where(second, jnp.where(here, rest, mid), rest2))
        pltpu.store(plane.at[pl.ds(z * ZROWS + 2 * tile, 8), :], v, mask=mask)


def each_other(me, action):
    step = 9

    @pl.loop(0, (NDEV - 2) // step)
    def _(t):
        for u in range(step):
            action((me + step * t + u + 1) & (NDEV - 1))

    action((me + NDEV - 1) & (NDEV - 1))


def device(d):
    return (d >> 6, d & (INNER - 1))


def send_all(me, msg, got, send_sem, recv_sem, h):
    def send(d):
        pltpu.make_async_remote_copy(
            src_ref=msg.at[h, pl.ds(pl.multiple_of(8 * d, 8), 8), :],
            dst_ref=got.at[h, pl.ds(pl.multiple_of(8 * me, 8), 8), :],
            send_sem=send_sem.at[h],
            recv_sem=recv_sem.at[h],
            device_id=device(d),
            device_id_type=MESH,
        ).start()

    each_other(me, send)


def own_copy(me, msg, got, sem, h):
    mine = pl.ds(pl.multiple_of(8 * me, 8), 8)
    return pltpu.make_async_copy(msg.at[h, mine, :], got.at[h, mine, :], sem.at[h])


def wait_bytes(buf, sem, h):
    part = buf.at[h, pl.ds(0, 8 * (NDEV - 1)), :]
    pltpu.make_async_copy(part, part, sem.at[h]).wait()


def prepare_base(deriv, table):
    @pl.loop(0, 17)
    def _(t):
        for u in range(17):
            n = 17 * t + u
            v = [deriv[n, :, pl.ds(128 * kc, 128)] for kc in range(3)]
            for h in range(2):
                v0, v1, v2 = (x[2 * h : 2 * h + 2] for x in v)
                table[h, n] = jnp.concatenate([v0, v0, v1, v1], axis=0)
                table[2 + h, n] = jnp.concatenate([v2, v2, v2, v2], axis=0)


def prepare_tables(table):
    row = lax.broadcasted_iota(jnp.int32, (8, 128), 0)

    @pl.loop(0, 4)
    def _(n):
        for slot, x, y in PLAN.level1:
            table[n, slot] = table[n, x] - table[n, y]
        for slot, x, y, z in PLAN.second:
            table[n, slot] = -(table[n, x] + table[n, y]) - table[n, z]

    @pl.loop(2, 4)
    def _(n):
        for own, other in PLAN.pairs:
            up = jnp.zeros((8, 128), F32) if other is None else table[n, other]
            table[n, own] = jnp.where(row < 4, table[n, own], up)

    @pl.loop(0, 4)
    def _(n):
        for slot, x, y in PLAN.level2:
            table[n, slot] = -table[n, y] if x is None else table[n, x] - table[n, y]


def gather_columns(got, xt, h, off):
    back = (128 - off) & 127
    for r in range(2):
        lanes = slice(128 * r, 128 * r + 128)
        for z in range(ZL):
            v = got[h, pl.ds(2 * z + r, NDEV, stride=8), :]
            xt[MROWS * z : MROWS * z + 128, lanes] = pltpu.roll(v, back, 1).T
        v = pltpu.roll(got[h, pl.ds(6 + r, NDEV, stride=8), :], back, 1).T
        for z in range(ZL):
            xt[MROWS * z + 128 : MROWS * z + HALF, lanes] = v[REST * z : REST * z + REST]


def product(x, w, first):
    high, low = split(x)
    dot = functools.partial(jnp.dot, preferred_element_type=F32)
    whigh, wlow = w[256 * first : 256 * first + 256, :], w[256 * first + 256 : 256 * first + 512, :]
    return dot(high, whigh) + dot(low, whigh) + dot(high, wlow)


def turned(turn, z, re, im, sign):
    if z == 0:
        return re, im
    c, s = turn[2 * z - 2 : 2 * z - 1, :], turn[2 * z - 1 : 2 * z, :] * sign
    return re * c - im * s, im * c + re * s


def triple(a, b, c, sign):
    sums = b[0] + c[0], b[1] + c[1]
    v = (b[0] - c[0]) * (ROOT * sign), (b[1] - c[1]) * (ROOT * sign)
    u = a[0] - 0.5 * sums[0], a[1] - 0.5 * sums[1]
    return (a[0] + sums[0], a[1] + sums[1]), (u[0] - v[1], u[1] + v[0]), (u[0] + v[1], u[1] - v[0])


def forward(xt, w, turn, sbuf):
    g = product(xt[...], w, 0)
    parts = []
    for z in range(ZL):
        at = MROWS * z
        parts.append(turned(turn, z, g[at : at + MROWS, 0:128], g[at : at + MROWS, 128:256], -1.0))
    for kc, value in enumerate(triple(*parts, -1.0)):
        for r in range(2):
            row = (2 * kc + r) * HALF
            sbuf[row : row + HALF, :] = value[r][:HALF]


def contract(table, n, stage, paired, finish, hold, gate):
    step = 2 if paired else 1
    inputs = {}
    spare = [COMP]

    def added(x, y):
        if y is None:
            return x
        stage[spare[0]] = stage[x] + stage[y]
        spare[0] += 1
        return spare[0] - 1

    part = [{}, {}]
    for c in range(2):
        for i in range(0, ORDER + 1 - c, step):
            for j in range(ORDER + 1 - c - i):
                part[c][i, j] = LOWER[i, j, c]
    inputs["a"], inputs["b"] = part
    inputs["p"] = {x: added(s, part[1].get(x)) for x, s in part[0].items()}
    leaves = {}
    for kind in "pab":
        even = {(i, j // 2): s for (i, j), s in inputs[kind].items() if j % 2 == 0}
        odd = {(i, j // 2): s for (i, j), s in inputs[kind].items() if j % 2 == 1}
        leaves[kind] = {"a": even, "b": odd, "p": {x: added(s, odd.get(x)) for x, s in even.items()}}

    def leaf_rows(kind, sub, counts):
        acc = {i: [None] * count for i, count in counts.items()}
        mine = {}
        for (i2, m2), slot in leaves[kind][sub].items():
            mine.setdefault(i2, []).append((m2, slot))
        loaded = {}
        for top in sorted({i + i2 for i in counts for i2 in mine}):
            seen = {}
            for i, count in counts.items():
                for m2, slot in mine.get(top - i, ()):
                    for m in range(count):
                        place = PLAN.two.get((kind, sub, top, m + m2))
                        if place is None:
                            continue
                        if slot not in loaded:
                            loaded[slot] = stage[slot]
                        if m + m2 not in seen:
                            seen[m + m2] = table[n, place]
                        v = seen[m + m2] * loaded[slot]
                        acc[i][m] = v if acc[i][m] is None else acc[i][m] + v
        return acc

    def rows_of(kind, counts):
        evens, odds = ({i: (count + e) // 2 for i, count in counts.items()} for e in (1, 0))
        p = leaf_rows(kind, "p", evens)
        a = leaf_rows(kind, "a", evens)
        b = leaf_rows(kind, "b", odds)
        out = {i: [None] * count for i, count in counts.items()}
        for i in counts:
            for m in range(evens[i]):
                out[i][2 * m] = a[i][m] if p[i][m] is None else p[i][m] + a[i][m]
            for m in range(odds[i]):
                out[i][2 * m + 1] = p[i][m] + b[i][m]
        return out

    left = list(range(ORDER + 1))
    while left:
        group = [i for i in (left[0], left[0] + step) if i in left]
        left = [i for i in left if i not in group]
        counts = {i: ORDER + 1 - i for i in group}
        place = {}
        for i in group:
            for j in range(counts[i]):
                place[i, j] = len(place)
        known = set()

        @pl.when(gate)
        def _():
            p = rows_of("p", counts)
            for (i, j), at in place.items():
                if p[i][j] is not None:
                    hold[at] = p[i][j]
                    known.add((i, j))

        @pl.when(gate)
        def _():
            a = rows_of("a", counts)
            for (i, j), at in place.items():
                finish(LOWER[i, j, 0], hold[at] + a[i][j] if (i, j) in known else a[i][j])

        @pl.when(gate)
        def _():
            b = rows_of("b", {i: count - 1 for i, count in counts.items()})
            for i in group:
                for j in range(counts[i] - 1):
                    finish(LOWER[i, j, 1], hold[place[i, j]] + b[i][j])


def contract_half(table, h, sbuf, stage, stage2, tbuf, hold, gate):
    row = lax.broadcasted_iota(jnp.int32, (8, 128), 0)
    for b in range(COMP):
        stage[b] = sbuf[pl.ds(b, 8, stride=COMP), :]
    for (i, j, c), b in LOWER.items():
        if i % 2 == 0:
            v = sbuf[pl.ds(8 * COMP + b, 8, stride=COMP), :]
            up = LOWER.get((i + 1, j, c))
            up = jnp.zeros((8, 128), F32) if up is None else sbuf[pl.ds(4 * COMP + up, 8, stride=COMP), :]
            stage2[b] = jnp.where(row < 4, v, up)

    def finish(a, v):
        tbuf[pl.ds(a, 8, stride=COMP), :] = v

    def finish2(a, v):
        tbuf[pl.ds(8 * COMP + a, 8, stride=COMP), :] = v + pltpu.roll(v, 4, 0)

    contract(table, h, stage, False, finish, hold, gate)
    contract(table, 2 + h, stage2, True, finish2, hold, gate)


def backward(tbuf, w, turn, ybuf):
    parts = []
    for kc in range(3):
        rows = [(2 * kc + r) * HALF for r in range(2)]
        parts.append(tuple(tbuf[row : row + MROWS, :] for row in rows))
    x = [turned(turn, z, *value, 1.0) for z, value in enumerate(triple(*parts, 1.0))]
    x = jnp.concatenate([jnp.concatenate(v, axis=1) for v in x], axis=0)
    ybuf[...] = product(x, w, 2)


def scatter_columns(ybuf, rest, msg, h, off):
    for r in range(2):
        lanes = slice(128 * r, 128 * r + 128)
        for z in range(ZL):
            at = MROWS * z
            msg[h, pl.ds(2 * z + r, NDEV, stride=8), :] = pltpu.roll(ybuf[at : at + 128, lanes].T, off, 1)
            rest[r, REST * z : REST * z + REST, :] = ybuf[at + 128 : at + HALF, lanes]
        msg[h, pl.ds(6 + r, NDEV, stride=8), :] = pltpu.roll(rest[r].T, off, 1)


def kernel(
    planes_hbm, deriv_hbm, w_hbm, out,
    plane, deriv, w, turn, table, msg, got, msg2, got2, xt, sbuf, stage, stage2, tbuf, hold, ybuf, rest,
    load_sem, own_sem, send_sem, recv_sem, own_sem2, send_sem2, recv_sem2,
):
    me = lax.axis_index("grp") * INNER + lax.axis_index("dev")
    loads = [
        pltpu.make_async_copy(planes_hbm, plane.at[pl.ds(LEAD, ZL * ZROWS), :], load_sem.at[0]),
        pltpu.make_async_copy(deriv_hbm, deriv, load_sem.at[1]),
        pltpu.make_async_copy(w_hbm.at[pl.ds(0, 1072), :], w, load_sem.at[2]),
    ]
    for copy in loads:
        copy.start()
    barrier = pltpu.get_barrier_semaphore()

    each_other(me, lambda d: pl.semaphore_signal(barrier, inc=1, device_id=device(d), device_id_type=MESH))
    plane[0:LEAD, :] = jnp.zeros((LEAD, 128), F32)
    plane[LEAD + ZL * ZROWS :, :] = jnp.zeros((16, 128), F32)
    loads[0].wait()

    for h in range(2):

        @pl.loop(0, NDEV, unroll=8)
        def _(d):
            pack(plane, msg, h, d)

    pl.semaphore_wait(barrier, NDEV - 1)
    for h in range(2):
        send_all(me, msg, got, send_sem, recv_sem, h)
        own_copy(me, msg, got, own_sem, h).start()
    for copy in loads[1:]:
        copy.wait()
    prepare_base(deriv, table)
    prepare_tables(table)
    small = [w[1024 + 16 * n : 1040 + 16 * n, 0:128].astype(F32) for n in range(3)]
    turn[...] = small[0] + (small[1] + small[2])
    xt[...] = jnp.zeros(xt.shape, F32)
    rest[...] = jnp.zeros(rest.shape, F32)
    @pl.loop(0, 2)
    def _(h):
        off = column_start(me, h)[1]
        own_copy(me, msg, got, own_sem, h).wait()
        wait_bytes(got, recv_sem, h)
        gather_columns(got, xt, h, off)
        forward(xt, w, turn, sbuf)
        contract_half(table, h, sbuf, stage, stage2, tbuf, hold, me >= 0)
        backward(tbuf, w, turn, ybuf)
        scatter_columns(ybuf, rest, msg2, h, off)
        send_all(me, msg2, got2, send_sem2, recv_sem2, h)
        own_copy(me, msg2, got2, own_sem2, h).start()

    for h in range(2):
        own_copy(me, msg2, got2, own_sem2, h).wait()
        wait_bytes(got2, recv_sem2, h)

        @pl.loop(0, NDEV, unroll=8)
        def _(s):
            unpack(got2, out, h, s)

    for h in range(2):
        wait_bytes(msg, send_sem, h)
        wait_bytes(msg2, send_sem2, h)


def on_device(multipoles, derivatives):
    planes = with_layout_constraint(multipoles.reshape(2, ZL, COLS, 128), Layout((1, 2, 0, 3)))
    planes = jnp.transpose(planes, (1, 2, 0, 3)).reshape(ZL * ZROWS, 128)
    deriv = jnp.transpose(derivatives, (2, 1, 0))
    vmem, dma = pltpu.VMEM, pltpu.SemaphoreType.DMA
    out = pl.pallas_call(
        kernel,
        out_shape=jax.ShapeDtypeStruct((OUT_ROWS, 128), F32),
        in_specs=[pl.BlockSpec(memory_space=pl.ANY)] * 3,
        out_specs=pl.BlockSpec(memory_space=pltpu.VMEM),
        scratch_shapes=[
            vmem((PLANE_ROWS, 128), F32),
            vmem((289, 4, NZ), F32),
            vmem((1072, 256), BF16),
            vmem((16, 128), F32),
            vmem((4, PLAN.count, 8, 128), F32),
            vmem((2, 8 * NDEV, 128), F32),
            vmem((2, 8 * NDEV, 128), F32),
            vmem((2, 8 * NDEV, 128), F32),
            vmem((2, 8 * NDEV, 128), F32),
            vmem((ZL * MROWS, 256), F32),
            vmem((16 * COMP, 128), F32),
            vmem((3 * COMP, 8, 128), F32),
            vmem((3 * COMP, 8, 128), F32),
            vmem((16 * COMP, 128), F32),
            vmem((24, 8, 128), F32),
            vmem((ZL * MROWS, 256), F32),
            vmem((2, 128, 128), F32),
            dma((4,)), dma((2,)), dma((2,)), dma((2,)), dma((2,)), dma((2,)), dma((2,)),
        ],
        compiler_params=pltpu.CompilerParams(
            collective_id=0, has_side_effects=True, vmem_limit_bytes=54300000
        ),
        name="m2l",
    )(planes, deriv, jnp.asarray(dft_tables()))
    out = jnp.transpose(out[: ZL * ZROWS].reshape(ZL, COLS, 2, 128), (0, 2, 1, 3)).reshape(ZL, 2, COLS * 128)
    return jnp.transpose(out, (1, 0, 2))


def solution(mesh):
    in_specs = (P(None, ("grp", "dev"), None), P(None, ("grp", "dev"), None))
    out_specs = P(None, ("grp", "dev"), None)
    return jax.shard_map(
        on_device, mesh=mesh, in_specs=in_specs, out_specs=out_specs, check_vma=False
    )
```

```python
import functools
import math

import jax
import jax.numpy as jnp
import ml_dtypes
import numpy as np
from jax import lax
from jax.experimental import pallas as pl
from jax.experimental.layout import Layout, with_layout_constraint
from jax.experimental.pallas import tpu as pltpu
from jax.sharding import PartitionSpec as P

ORDER = 8
MESH = pl.DeviceIdType.MESH
F32 = jnp.float32
BF16 = jnp.bfloat16

COMP = 81
NDEV = 128
INNER = 64
NZ = 384
ZL = 3
COLS = 324
HALF = 162
REST = 34
MROWS = 168
ROOT = math.sqrt(3.0) / 2
ZROWS = 648
LEAD = 8
OUT_ROWS = ZL * ZROWS + 8
PLANE_ROWS = LEAD + ZL * ZROWS + 16


def reduced_terms(highest):
    listed = []
    for total in range(highest + 1):
        for upper in range(min(total, 1) + 1):
            for first in range(total - upper, -1, -1):
                listed.append((first, total - upper - first, upper))
    return listed


LOWER = {t: n for n, t in enumerate(reduced_terms(ORDER))}
HIGHER = {t: n for n, t in enumerate(reduced_terms(2 * ORDER))}


class Plan:
    def __init__(self):
        self.count = len(HIGHER)
        self.second, self.level1, self.level2 = [], [], []
        self.pairs = []
        self.one = {}
        top = 2 * ORDER
        for total in range(top + 1):
            for i in range(total + 1):
                j = total - i
                d0, d1 = HIGHER[i, j, 0], HIGHER.get((i, j, 1))
                self.one["p", i, j] = d1
                self.one["a", i, j] = d0
                if d1 is not None:
                    self.one["a", i, j] = self.fresh()
                    self.level1.append((self.one["a", i, j], d0, d1))
                self.one["b", i, j] = None
                if total <= top - 2:
                    self.one["b", i, j] = self.fresh()
                    self.second.append((self.one["b", i, j], HIGHER[i + 2, j, 0], HIGHER[i, j + 2, 0], d1))
        for total in range(top + 1):
            for i in range(total + 1):
                for kind in "pab":
                    own, other = self.one[kind, i, total - i], self.one.get((kind, i + 1, total - i))
                    if own is not None:
                        self.pairs.append((own, other))
        self.two = {}
        for kind in "pab":
            for i in range(top + 1):
                for m in range(ORDER + 1):
                    even, odd, after = (self.one.get((kind, i, 2 * m + e)) for e in range(3))
                    self.two[kind, "p", i, m] = odd
                    self.two[kind, "a", i, m] = self.minus(even, odd)
                    self.two[kind, "b", i, m] = self.minus(after, odd)

    def fresh(self):
        self.count += 1
        return self.count - 1

    def minus(self, x, y):
        if y is None:
            return x
        slot = self.fresh()
        self.level2.append((slot, x, y))
        return slot


PLAN = Plan()


def dft_tables():
    n = np.arange(NDEV)
    angle = 2.0 * np.pi / NDEV * (n[:, None] * n[None, :] % NDEV)
    c, s = np.cos(angle) / math.sqrt(NZ), np.sin(angle) / math.sqrt(NZ)
    out = []
    for w in (np.block([[c, -s], [s, c]]), np.block([[c, s], [-s, c]])):
        high = w.astype(ml_dtypes.bfloat16)
        out += [high, (w - high.astype(np.float64)).astype(ml_dtypes.bfloat16)]
    rows = np.concatenate(out + turn_rows())
    return np.pad(rows, ((0, 5120 - len(rows)), (0, 0)))


def turn_rows():
    angle = 2.0 * np.pi / NZ * np.arange(NDEV)
    left = np.zeros((16, 256))
    left[:4, :NDEV] = [f(z * angle) for z in (1, 2) for f in (np.cos, np.sin)]
    out = []
    for _ in range(3):
        out.append(left.astype(ml_dtypes.bfloat16))
        left = left - out[-1].astype(np.float64)
    return out


def split(x):
    high = x.astype(BF16)
    return high, (x - high.astype(F32)).astype(BF16)


def iotas():
    lane = lax.broadcasted_iota(jnp.int32, (8, 128), 1)
    row = lax.broadcasted_iota(jnp.int32, (8, 128), 0)
    return lane, row


def column_start(owner, h):
    start = COLS * owner + HALF * h
    return start >> 7, start & 127


def pack(plane, msg, h, d):
    lane, row = iotas()
    tile, off = column_start(d, h)
    here = lane >= off
    rel = jnp.where(here, lane - off, lane - off + 128)
    main = rest = None
    for z in range(ZL):
        at = LEAD + z * ZROWS + 2 * tile - 2 * z
        v = jnp.where(here, plane[pl.ds(at, 8), :], plane[pl.ds(at + 2, 8), :])
        main = v if z == 0 else jnp.where(row >= 2 * z, v, main)
        at = LEAD + z * ZROWS + 2 * tile - 4
        v = jnp.where(here, plane[pl.ds(at, 8), :], plane[pl.ds(at + 2, 8), :])
        if z:
            v = pltpu.roll(v, REST * z, 1)
        rest = v if z == 0 else jnp.where(rel >= REST * z, v, rest)
    msg[h, pl.ds(pl.multiple_of(8 * d, 8), 8), :] = jnp.where(row >= 6, rest, main)


def unpack(got, plane, h, s):
    lane, row = iotas()
    tile, off = column_start(s, h)
    here = lane >= off
    column = (row >> 1) * 128 + lane - off
    mask = (column >= 0) & (column < HALF)
    first, second = row < 2, row < 4
    m = got[h, pl.ds(pl.multiple_of(8 * s, 8), 8), :]
    down, up, up2 = pltpu.roll(m, 2, 0), pltpu.roll(m, 6, 0), pltpu.roll(m, 4, 0)
    for z, (top, mid) in enumerate(((m, down), (up, m), (up2, up))):
        rest, rest2 = up2, up
        if z:
            rest, rest2 = pltpu.roll(up2, 128 - REST * z, 1), pltpu.roll(up, 128 - REST * z, 1)
        v = jnp.where(first, top, jnp.where(second, jnp.where(here, rest, mid), rest2))
        pltpu.store(plane.at[pl.ds(z * ZROWS + 2 * tile, 8), :], v, mask=mask)


def each_other(me, action):
    step = 9

    @pl.loop(0, (NDEV - 2) // step)
    def _(t):
        for u in range(step):
            action((me + step * t + u + 1) & (NDEV - 1))

    action((me + NDEV - 1) & (NDEV - 1))


def device(d):
    return (d >> 6, d & (INNER - 1))


def send_all(me, msg, got, send_sem, recv_sem, h):
    def send(d):
        pltpu.make_async_remote_copy(
            src_ref=msg.at[h, pl.ds(pl.multiple_of(8 * d, 8), 8), :],
            dst_ref=got.at[h, pl.ds(pl.multiple_of(8 * me, 8), 8), :],
            send_sem=send_sem.at[h],
            recv_sem=recv_sem.at[h],
            device_id=device(d),
            device_id_type=MESH,
        ).start()

    each_other(me, send)


def own_copy(me, msg, got, sem, h):
    mine = pl.ds(pl.multiple_of(8 * me, 8), 8)
    return pltpu.make_async_copy(msg.at[h, mine, :], got.at[h, mine, :], sem.at[h])


def wait_bytes(buf, sem, h):
    part = buf.at[h, pl.ds(0, 8 * (NDEV - 1)), :]
    pltpu.make_async_copy(part, part, sem.at[h]).wait()


def prepare_base(deriv, table):
    @pl.loop(0, 17)
    def _(t):
        for u in range(17):
            n = 17 * t + u
            v = [deriv[n, :, pl.ds(128 * kc, 128)] for kc in range(3)]
            for h in range(2):
                v0, v1, v2 = (x[2 * h : 2 * h + 2] for x in v)
                table[h, n] = jnp.concatenate([v0, v0, v1, v1], axis=0)
                table[2 + h, n] = jnp.concatenate([v2, v2, v2, v2], axis=0)


def prepare_tables(table):
    row = lax.broadcasted_iota(jnp.int32, (8, 128), 0)

    @pl.loop(0, 4)
    def _(n):
        for slot, x, y in PLAN.level1:
            table[n, slot] = table[n, x] - table[n, y]
        for slot, x, y, z in PLAN.second:
            table[n, slot] = -(table[n, x] + table[n, y]) - table[n, z]

    @pl.loop(2, 4)
    def _(n):
        for own, other in PLAN.pairs:
            up = jnp.zeros((8, 128), F32) if other is None else table[n, other]
            table[n, own] = jnp.where(row < 4, table[n, own], up)

    @pl.loop(0, 4)
    def _(n):
        for slot, x, y in PLAN.level2:
            table[n, slot] = -table[n, y] if x is None else table[n, x] - table[n, y]


def gather_columns(got, xt, h, off):
    back = (128 - off) & 127
    for r in range(2):
        lanes = slice(128 * r, 128 * r + 128)
        for z in range(ZL):
            v = got[h, pl.ds(2 * z + r, NDEV, stride=8), :]
            xt[MROWS * z : MROWS * z + 128, lanes] = pltpu.roll(v, back, 1).T
        v = pltpu.roll(got[h, pl.ds(6 + r, NDEV, stride=8), :], back, 1).T
        for z in range(ZL):
            xt[MROWS * z + 128 : MROWS * z + HALF, lanes] = v[REST * z : REST * z + REST]


def product(x, w, first):
    high, low = split(x)
    dot = functools.partial(jnp.dot, preferred_element_type=F32)
    whigh, wlow = w[256 * first : 256 * first + 256, :], w[256 * first + 256 : 256 * first + 512, :]
    return dot(high, whigh) + dot(low, whigh) + dot(high, wlow)


def turned(turn, z, re, im, sign):
    if z == 0:
        return re, im
    c, s = turn[2 * z - 2 : 2 * z - 1, :], turn[2 * z - 1 : 2 * z, :] * sign
    return re * c - im * s, im * c + re * s


def triple(a, b, c, sign):
    sums = b[0] + c[0], b[1] + c[1]
    v = (b[0] - c[0]) * (ROOT * sign), (b[1] - c[1]) * (ROOT * sign)
    u = a[0] - 0.5 * sums[0], a[1] - 0.5 * sums[1]
    return (a[0] + sums[0], a[1] + sums[1]), (u[0] - v[1], u[1] + v[0]), (u[0] + v[1], u[1] - v[0])


def forward(xt, w, turn, sbuf):
    g = product(xt[...], w, 0)
    parts = []
    for z in range(ZL):
        at = MROWS * z
        parts.append(turned(turn, z, g[at : at + MROWS, 0:128], g[at : at + MROWS, 128:256], -1.0))
    for kc, value in enumerate(triple(*parts, -1.0)):
        for r in range(2):
            row = (2 * kc + r) * HALF
            sbuf[row : row + HALF, :] = value[r][:HALF]


def contract(table, n, stage, paired, finish, hold, gate):
    step = 2 if paired else 1
    inputs = {}
    spare = [COMP]

    def added(x, y):
        if y is None:
            return x
        stage[spare[0]] = stage[x] + stage[y]
        spare[0] += 1
        return spare[0] - 1

    part = [{}, {}]
    for c in range(2):
        for i in range(0, ORDER + 1 - c, step):
            for j in range(ORDER + 1 - c - i):
                part[c][i, j] = LOWER[i, j, c]
    inputs["a"], inputs["b"] = part
    inputs["p"] = {x: added(s, part[1].get(x)) for x, s in part[0].items()}
    leaves = {}
    for kind in "pab":
        even = {(i, j // 2): s for (i, j), s in inputs[kind].items() if j % 2 == 0}
        odd = {(i, j // 2): s for (i, j), s in inputs[kind].items() if j % 2 == 1}
        leaves[kind] = {"a": even, "b": odd, "p": {x: added(s, odd.get(x)) for x, s in even.items()}}

    def leaf_rows(kind, sub, counts):
        acc = {i: [None] * count for i, count in counts.items()}
        mine = {}
        for (i2, m2), slot in leaves[kind][sub].items():
            mine.setdefault(i2, []).append((m2, slot))
        loaded = {}
        for top in sorted({i + i2 for i in counts for i2 in mine}):
            seen = {}
            for i, count in counts.items():
                for m2, slot in mine.get(top - i, ()):
                    for m in range(count):
                        place = PLAN.two.get((kind, sub, top, m + m2))
                        if place is None:
                            continue
                        if slot not in loaded:
                            loaded[slot] = stage[slot]
                        if m + m2 not in seen:
                            seen[m + m2] = table[n, place]
                        v = seen[m + m2] * loaded[slot]
                        acc[i][m] = v if acc[i][m] is None else acc[i][m] + v
        return acc

    def rows_of(kind, counts):
        evens, odds = ({i: (count + e) // 2 for i, count in counts.items()} for e in (1, 0))
        p = leaf_rows(kind, "p", evens)
        a = leaf_rows(kind, "a", evens)
        b = leaf_rows(kind, "b", odds)
        out = {i: [None] * count for i, count in counts.items()}
        for i in counts:
            for m in range(evens[i]):
                out[i][2 * m] = a[i][m] if p[i][m] is None else p[i][m] + a[i][m]
            for m in range(odds[i]):
                out[i][2 * m + 1] = p[i][m] + b[i][m]
        return out

    left = list(range(ORDER + 1))
    while left:
        group = [i for i in (left[0], left[0] + step) if i in left]
        left = [i for i in left if i not in group]
        counts = {i: ORDER + 1 - i for i in group}
        place = {}
        for i in group:
            for j in range(counts[i]):
                place[i, j] = len(place)
        known = set()

        @pl.when(gate)
        def _():
            p = rows_of("p", counts)
            for (i, j), at in place.items():
                if p[i][j] is not None:
                    hold[at] = p[i][j]
                    known.add((i, j))

        @pl.when(gate)
        def _():
            a = rows_of("a", counts)
            for (i, j), at in place.items():
                finish(LOWER[i, j, 0], hold[at] + a[i][j] if (i, j) in known else a[i][j])

        @pl.when(gate)
        def _():
            b = rows_of("b", {i: count - 1 for i, count in counts.items()})
            for i in group:
                for j in range(counts[i] - 1):
                    finish(LOWER[i, j, 1], hold[place[i, j]] + b[i][j])


def contract_half(table, h, sbuf, stage, stage2, tbuf, hold, gate):
    row = lax.broadcasted_iota(jnp.int32, (8, 128), 0)
    for b in range(COMP):
        stage[b] = sbuf[pl.ds(b, 8, stride=COMP), :]
    for (i, j, c), b in LOWER.items():
        if i % 2 == 0:
            v = sbuf[pl.ds(8 * COMP + b, 8, stride=COMP), :]
            up = LOWER.get((i + 1, j, c))
            up = jnp.zeros((8, 128), F32) if up is None else sbuf[pl.ds(4 * COMP + up, 8, stride=COMP), :]
            stage2[b] = jnp.where(row < 4, v, up)

    def finish(a, v):
        tbuf[pl.ds(a, 8, stride=COMP), :] = v

    def finish2(a, v):
        tbuf[pl.ds(8 * COMP + a, 8, stride=COMP), :] = v + pltpu.roll(v, 4, 0)

    contract(table, h, stage, False, finish, hold, gate)
    contract(table, 2 + h, stage2, True, finish2, hold, gate)


def backward(tbuf, w, turn, ybuf):
    parts = []
    for kc in range(3):
        rows = [(2 * kc + r) * HALF for r in range(2)]
        parts.append(tuple(tbuf[row : row + MROWS, :] for row in rows))
    x = [turned(turn, z, *value, 1.0) for z, value in enumerate(triple(*parts, 1.0))]
    x = jnp.concatenate([jnp.concatenate(v, axis=1) for v in x], axis=0)
    ybuf[...] = product(x, w, 2)


def scatter_columns(ybuf, rest, msg, h, off):
    for r in range(2):
        lanes = slice(128 * r, 128 * r + 128)
        for z in range(ZL):
            at = MROWS * z
            msg[h, pl.ds(2 * z + r, NDEV, stride=8), :] = pltpu.roll(ybuf[at : at + 128, lanes].T, off, 1)
            rest[r, REST * z : REST * z + REST, :] = ybuf[at + 128 : at + HALF, lanes]
        msg[h, pl.ds(6 + r, NDEV, stride=8), :] = pltpu.roll(rest[r].T, off, 1)


def kernel(
    planes_hbm, deriv_hbm, w_hbm, out,
    plane, deriv, w, turn, table, msg, got, msg2, got2, xt, sbuf, stage, stage2, tbuf, hold, ybuf, rest,
    load_sem, own_sem, send_sem, recv_sem, own_sem2, send_sem2, recv_sem2,
):
    me = lax.axis_index("grp") * INNER + lax.axis_index("dev")
    loads = [
        pltpu.make_async_copy(planes_hbm, plane.at[pl.ds(LEAD, ZL * ZROWS), :], load_sem.at[0]),
        pltpu.make_async_copy(deriv_hbm, deriv, load_sem.at[1]),
        pltpu.make_async_copy(w_hbm.at[pl.ds(0, 1072), :], w, load_sem.at[2]),
    ]
    for copy in loads:
        copy.start()
    barrier = pltpu.get_barrier_semaphore()

    each_other(me, lambda d: pl.semaphore_signal(barrier, inc=1, device_id=device(d), device_id_type=MESH))
    plane[0:LEAD, :] = jnp.zeros((LEAD, 128), F32)
    plane[LEAD + ZL * ZROWS :, :] = jnp.zeros((16, 128), F32)
    loads[0].wait()

    for h in range(2):

        @pl.loop(0, NDEV, unroll=8)
        def _(d):
            pack(plane, msg, h, d)

    pl.semaphore_wait(barrier, NDEV - 1)
    for h in range(2):
        send_all(me, msg, got, send_sem, recv_sem, h)
        own_copy(me, msg, got, own_sem, h).start()
    for copy in loads[1:]:
        copy.wait()
    prepare_base(deriv, table)
    prepare_tables(table)
    small = [w[1024 + 16 * n : 1040 + 16 * n, 0:128].astype(F32) for n in range(3)]
    turn[...] = small[0] + (small[1] + small[2])
    xt[...] = jnp.zeros(xt.shape, F32)
    rest[...] = jnp.zeros(rest.shape, F32)
    @pl.loop(0, 2)
    def _(h):
        off = column_start(me, h)[1]
        own_copy(me, msg, got, own_sem, h).wait()
        wait_bytes(got, recv_sem, h)
        gather_columns(got, xt, h, off)
        forward(xt, w, turn, sbuf)
        contract_half(table, h, sbuf, stage, stage2, tbuf, hold, me >= 0)
        backward(tbuf, w, turn, ybuf)
        scatter_columns(ybuf, rest, msg2, h, off)
        send_all(me, msg2, got2, send_sem2, recv_sem2, h)
        own_copy(me, msg2, got2, own_sem2, h).start()

    for h in range(2):
        own_copy(me, msg2, got2, own_sem2, h).wait()
        wait_bytes(got2, recv_sem2, h)

        @pl.loop(0, NDEV, unroll=8)
        def _(s):
            unpack(got2, out, h, s)

    for h in range(2):
        wait_bytes(msg, send_sem, h)
        wait_bytes(msg2, send_sem2, h)


def on_device(multipoles, derivatives):
    planes = with_layout_constraint(multipoles.reshape(2, ZL, COLS, 128), Layout((1, 2, 0, 3)))
    planes = jnp.transpose(planes, (1, 2, 0, 3)).reshape(ZL * ZROWS, 128)
    deriv = jnp.transpose(derivatives, (2, 1, 0))
    vmem, dma = pltpu.VMEM, pltpu.SemaphoreType.DMA
    out = pl.pallas_call(
        kernel,
        out_shape=pltpu.VMEM((OUT_ROWS, 128), F32),
        in_specs=[pl.BlockSpec(memory_space=pl.ANY)] * 3,
        out_specs=pl.BlockSpec(memory_space=pltpu.VMEM),
        scratch_shapes=[
            vmem((PLANE_ROWS, 128), F32),
            vmem((289, 4, NZ), F32),
            vmem((1072, 256), BF16),
            vmem((16, 128), F32),
            vmem((4, PLAN.count, 8, 128), F32),
            vmem((2, 8 * NDEV, 128), F32),
            vmem((2, 8 * NDEV, 128), F32),
            vmem((2, 8 * NDEV, 128), F32),
            vmem((2, 8 * NDEV, 128), F32),
            vmem((ZL * MROWS, 256), F32),
            vmem((16 * COMP, 128), F32),
            vmem((3 * COMP, 8, 128), F32),
            vmem((3 * COMP, 8, 128), F32),
            vmem((16 * COMP, 128), F32),
            vmem((24, 8, 128), F32),
            vmem((ZL * MROWS, 256), F32),
            vmem((2, 128, 128), F32),
            dma((4,)), dma((2,)), dma((2,)), dma((2,)), dma((2,)), dma((2,)), dma((2,)),
        ],
        compiler_params=pltpu.CompilerParams(
            collective_id=0, has_side_effects=True, vmem_limit_bytes=55000000
        ),
        name="m2l",
    )(planes, deriv, jnp.asarray(dft_tables()))
    out = jnp.transpose(out[: ZL * ZROWS].reshape(ZL, COLS, 2, 128), (0, 2, 1, 3)).reshape(ZL, 2, COLS * 128)
    return jnp.transpose(out, (1, 0, 2))


def solution(mesh):
    in_specs = (P(None, ("grp", "dev"), None), P(None, ("grp", "dev"), None))
    out_specs = P(None, ("grp", "dev"), None)
    return jax.shard_map(
        on_device, mesh=mesh, in_specs=in_specs, out_specs=out_specs, check_vma=False
    )
```

```python
import functools
import math

import jax
import jax.numpy as jnp
import ml_dtypes
import numpy as np
from jax import lax
from jax.experimental import pallas as pl
from jax.experimental.layout import Layout, with_layout_constraint
from jax.experimental.pallas import tpu as pltpu
from jax.sharding import PartitionSpec as P

ORDER = 8
MESH = pl.DeviceIdType.MESH
F32 = jnp.float32
BF16 = jnp.bfloat16

COMP = 81
NDEV = 128
INNER = 64
NZ = 384
ZL = 3
COLS = 324
HALF = 162
REST = 34
MROWS = 168
ROOT = math.sqrt(3.0) / 2
ZROWS = 648
LEAD = 8
OUT_ROWS = ZL * ZROWS + 8
PLANE_ROWS = LEAD + ZL * ZROWS + 16


def reduced_terms(highest):
    listed = []
    for total in range(highest + 1):
        for upper in range(min(total, 1) + 1):
            for first in range(total - upper, -1, -1):
                listed.append((first, total - upper - first, upper))
    return listed


LOWER = {t: n for n, t in enumerate(reduced_terms(ORDER))}
HIGHER = {t: n for n, t in enumerate(reduced_terms(2 * ORDER))}


class Plan:
    def __init__(self):
        self.count = len(HIGHER)
        self.second, self.level1, self.level2 = [], [], []
        self.pairs = []
        self.one = {}
        top = 2 * ORDER
        for total in range(top + 1):
            for i in range(total + 1):
                j = total - i
                d0, d1 = HIGHER[i, j, 0], HIGHER.get((i, j, 1))
                self.one["p", i, j] = d1
                self.one["a", i, j] = d0
                if d1 is not None:
                    self.one["a", i, j] = self.fresh()
                    self.level1.append((self.one["a", i, j], d0, d1))
                self.one["b", i, j] = None
                if total <= top - 2:
                    self.one["b", i, j] = self.fresh()
                    self.second.append((self.one["b", i, j], HIGHER[i + 2, j, 0], HIGHER[i, j + 2, 0], d1))
        for total in range(top + 1):
            for i in range(total + 1):
                for kind in "pab":
                    own, other = self.one[kind, i, total - i], self.one.get((kind, i + 1, total - i))
                    if own is not None:
                        self.pairs.append((own, other))
        self.two = {}
        for kind in "pab":
            for i in range(top + 1):
                for m in range(ORDER + 1):
                    even, odd, after = (self.one.get((kind, i, 2 * m + e)) for e in range(3))
                    self.two[kind, "p", i, m] = odd
                    self.two[kind, "a", i, m] = self.minus(even, odd)
                    self.two[kind, "b", i, m] = self.minus(after, odd)

    def fresh(self):
        self.count += 1
        return self.count - 1

    def minus(self, x, y):
        if y is None:
            return x
        slot = self.fresh()
        self.level2.append((slot, x, y))
        return slot


PLAN = Plan()


def dft_tables():
    n = np.arange(NDEV)
    angle = 2.0 * np.pi / NDEV * (n[:, None] * n[None, :] % NDEV)
    c, s = np.cos(angle) / math.sqrt(NZ), np.sin(angle) / math.sqrt(NZ)
    out = []
    for w in (np.block([[c, -s], [s, c]]), np.block([[c, s], [-s, c]])):
        high = w.astype(ml_dtypes.bfloat16)
        out += [high, (w - high.astype(np.float64)).astype(ml_dtypes.bfloat16)]
    rows = np.concatenate(out + turn_rows())
    return np.pad(rows, ((0, 5120 - len(rows)), (0, 0)))


def turn_rows():
    angle = 2.0 * np.pi / NZ * np.arange(NDEV)
    left = np.zeros((16, 256))
    left[:4, :NDEV] = [f(z * angle) for z in (1, 2) for f in (np.cos, np.sin)]
    out = []
    for _ in range(3):
        out.append(left.astype(ml_dtypes.bfloat16))
        left = left - out[-1].astype(np.float64)
    return out


def split(x):
    high = x.astype(BF16)
    return high, (x - high.astype(F32)).astype(BF16)


def iotas():
    lane = lax.broadcasted_iota(jnp.int32, (8, 128), 1)
    row = lax.broadcasted_iota(jnp.int32, (8, 128), 0)
    return lane, row


def column_start(owner, h):
    start = COLS * owner + HALF * h
    return start >> 7, start & 127


def pack(plane, msg, h, d):
    lane, row = iotas()
    tile, off = column_start(d, h)
    here = lane >= off
    rel = jnp.where(here, lane - off, lane - off + 128)
    main = rest = None
    for z in range(ZL):
        at = LEAD + z * ZROWS + 2 * tile - 2 * z
        v = jnp.where(here, plane[pl.ds(at, 8), :], plane[pl.ds(at + 2, 8), :])
        main = v if z == 0 else jnp.where(row >= 2 * z, v, main)
        at = LEAD + z * ZROWS + 2 * tile - 4
        v = jnp.where(here, plane[pl.ds(at, 8), :], plane[pl.ds(at + 2, 8), :])
        if z:
            v = pltpu.roll(v, REST * z, 1)
        rest = v if z == 0 else jnp.where(rel >= REST * z, v, rest)
    msg[h, pl.ds(pl.multiple_of(8 * d, 8), 8), :] = jnp.where(row >= 6, rest, main)


def unpack(got, plane, h, s):
    lane, row = iotas()
    tile, off = column_start(s, h)
    here = lane >= off
    column = (row >> 1) * 128 + lane - off
    mask = (column >= 0) & (column < HALF)
    first, second = row < 2, row < 4
    m = got[h, pl.ds(pl.multiple_of(8 * s, 8), 8), :]
    down, up, up2 = pltpu.roll(m, 2, 0), pltpu.roll(m, 6, 0), pltpu.roll(m, 4, 0)
    for z, (top, mid) in enumerate(((m, down), (up, m), (up2, up))):
        rest, rest2 = up2, up
        if z:
            rest, rest2 = pltpu.roll(up2, 128 - REST * z, 1), pltpu.roll(up, 128 - REST * z, 1)
        v = jnp.where(first, top, jnp.where(second, jnp.where(here, rest, mid), rest2))
        pltpu.store(plane.at[pl.ds(z * ZROWS + 2 * tile, 8), :], v, mask=mask)


def each_other(me, action):
    step = 9

    @pl.loop(0, (NDEV - 2) // step)
    def _(t):
        for u in range(step):
            action((me + 37 * (step * t + u + 1)) & (NDEV - 1))

    action((me - 37) & (NDEV - 1))


def device(d):
    return (d >> 6, d & (INNER - 1))


def send_all(me, msg, got, send_sem, recv_sem, h):
    def send(d):
        pltpu.make_async_remote_copy(
            src_ref=msg.at[h, pl.ds(pl.multiple_of(8 * d, 8), 8), :],
            dst_ref=got.at[h, pl.ds(pl.multiple_of(8 * me, 8), 8), :],
            send_sem=send_sem.at[h],
            recv_sem=recv_sem.at[h],
            device_id=device(d),
            device_id_type=MESH,
        ).start()

    each_other(me, send)


def own_copy(me, msg, got, sem, h):
    mine = pl.ds(pl.multiple_of(8 * me, 8), 8)
    return pltpu.make_async_copy(msg.at[h, mine, :], got.at[h, mine, :], sem.at[h])


def wait_bytes(buf, sem, h):
    part = buf.at[h, pl.ds(0, 8 * (NDEV - 1)), :]
    pltpu.make_async_copy(part, part, sem.at[h]).wait()


def prepare_base(deriv, table):
    @pl.loop(0, 17)
    def _(t):
        for u in range(17):
            n = 17 * t + u
            v = [deriv[n, :, pl.ds(128 * kc, 128)] for kc in range(3)]
            for h in range(2):
                v0, v1, v2 = (x[2 * h : 2 * h + 2] for x in v)
                table[h, n] = jnp.concatenate([v0, v0, v1, v1], axis=0)
                table[2 + h, n] = jnp.concatenate([v2, v2, v2, v2], axis=0)


def prepare_tables(table):
    row = lax.broadcasted_iota(jnp.int32, (8, 128), 0)

    @pl.loop(0, 4)
    def _(n):
        for slot, x, y in PLAN.level1:
            table[n, slot] = table[n, x] - table[n, y]
        for slot, x, y, z in PLAN.second:
            table[n, slot] = -(table[n, x] + table[n, y]) - table[n, z]

    @pl.loop(2, 4)
    def _(n):
        for own, other in PLAN.pairs:
            up = jnp.zeros((8, 128), F32) if other is None else table[n, other]
            table[n, own] = jnp.where(row < 4, table[n, own], up)

    @pl.loop(0, 4)
    def _(n):
        for slot, x, y in PLAN.level2:
            table[n, slot] = -table[n, y] if x is None else table[n, x] - table[n, y]


def gather_columns(got, xt, h, off):
    back = (128 - off) & 127
    for r in range(2):
        lanes = slice(128 * r, 128 * r + 128)
        for z in range(ZL):
            v = got[h, pl.ds(2 * z + r, NDEV, stride=8), :]
            xt[MROWS * z : MROWS * z + 128, lanes] = pltpu.roll(v, back, 1).T
        v = pltpu.roll(got[h, pl.ds(6 + r, NDEV, stride=8), :], back, 1).T
        for z in range(ZL):
            xt[MROWS * z + 128 : MROWS * z + HALF, lanes] = v[REST * z : REST * z + REST]


def product(x, w, first):
    high, low = split(x)
    dot = functools.partial(jnp.dot, preferred_element_type=F32)
    whigh, wlow = w[256 * first : 256 * first + 256, :], w[256 * first + 256 : 256 * first + 512, :]
    return dot(high, whigh) + dot(low, whigh) + dot(high, wlow)


def turned(turn, z, re, im, sign):
    if z == 0:
        return re, im
    c, s = turn[2 * z - 2 : 2 * z - 1, :], turn[2 * z - 1 : 2 * z, :] * sign
    return re * c - im * s, im * c + re * s


def triple(a, b, c, sign):
    sums = b[0] + c[0], b[1] + c[1]
    v = (b[0] - c[0]) * (ROOT * sign), (b[1] - c[1]) * (ROOT * sign)
    u = a[0] - 0.5 * sums[0], a[1] - 0.5 * sums[1]
    return (a[0] + sums[0], a[1] + sums[1]), (u[0] - v[1], u[1] + v[0]), (u[0] + v[1], u[1] - v[0])


def forward(xt, w, turn, sbuf):
    g = product(xt[...], w, 0)
    parts = []
    for z in range(ZL):
        at = MROWS * z
        parts.append(turned(turn, z, g[at : at + MROWS, 0:128], g[at : at + MROWS, 128:256], -1.0))
    for kc, value in enumerate(triple(*parts, -1.0)):
        for r in range(2):
            row = (2 * kc + r) * HALF
            sbuf[row : row + HALF, :] = value[r][:HALF]


def contract(table, n, stage, paired, finish, hold, gate):
    step = 2 if paired else 1
    inputs = {}
    spare = [COMP]

    def added(x, y):
        if y is None:
            return x
        stage[spare[0]] = stage[x] + stage[y]
        spare[0] += 1
        return spare[0] - 1

    part = [{}, {}]
    for c in range(2):
        for i in range(0, ORDER + 1 - c, step):
            for j in range(ORDER + 1 - c - i):
                part[c][i, j] = LOWER[i, j, c]
    inputs["a"], inputs["b"] = part
    inputs["p"] = {x: added(s, part[1].get(x)) for x, s in part[0].items()}
    leaves = {}
    for kind in "pab":
        even = {(i, j // 2): s for (i, j), s in inputs[kind].items() if j % 2 == 0}
        odd = {(i, j // 2): s for (i, j), s in inputs[kind].items() if j % 2 == 1}
        leaves[kind] = {"a": even, "b": odd, "p": {x: added(s, odd.get(x)) for x, s in even.items()}}

    def leaf_rows(kind, sub, counts):
        acc = {i: [None] * count for i, count in counts.items()}
        mine = {}
        for (i2, m2), slot in leaves[kind][sub].items():
            mine.setdefault(i2, []).append((m2, slot))
        loaded = {}
        for top in sorted({i + i2 for i in counts for i2 in mine}):
            seen = {}
            for i, count in counts.items():
                for m2, slot in mine.get(top - i, ()):
                    for m in range(count):
                        place = PLAN.two.get((kind, sub, top, m + m2))
                        if place is None:
                            continue
                        if slot not in loaded:
                            loaded[slot] = stage[slot]
                        if m + m2 not in seen:
                            seen[m + m2] = table[n, place]
                        v = seen[m + m2] * loaded[slot]
                        acc[i][m] = v if acc[i][m] is None else acc[i][m] + v
        return acc

    def rows_of(kind, counts):
        evens, odds = ({i: (count + e) // 2 for i, count in counts.items()} for e in (1, 0))
        p = leaf_rows(kind, "p", evens)
        a = leaf_rows(kind, "a", evens)
        b = leaf_rows(kind, "b", odds)
        out = {i: [None] * count for i, count in counts.items()}
        for i in counts:
            for m in range(evens[i]):
                out[i][2 * m] = a[i][m] if p[i][m] is None else p[i][m] + a[i][m]
            for m in range(odds[i]):
                out[i][2 * m + 1] = p[i][m] + b[i][m]
        return out

    left = list(range(ORDER + 1))
    while left:
        group = [i for i in (left[0], left[0] + step) if i in left]
        left = [i for i in left if i not in group]
        counts = {i: ORDER + 1 - i for i in group}
        place = {}
        for i in group:
            for j in range(counts[i]):
                place[i, j] = len(place)
        known = set()

        @pl.when(gate)
        def _():
            p = rows_of("p", counts)
            for (i, j), at in place.items():
                if p[i][j] is not None:
                    hold[at] = p[i][j]
                    known.add((i, j))

        @pl.when(gate)
        def _():
            a = rows_of("a", counts)
            for (i, j), at in place.items():
                finish(LOWER[i, j, 0], hold[at] + a[i][j] if (i, j) in known else a[i][j])

        @pl.when(gate)
        def _():
            b = rows_of("b", {i: count - 1 for i, count in counts.items()})
            for i in group:
                for j in range(counts[i] - 1):
                    finish(LOWER[i, j, 1], hold[place[i, j]] + b[i][j])


def contract_half(table, h, sbuf, stage, stage2, tbuf, hold, gate):
    row = lax.broadcasted_iota(jnp.int32, (8, 128), 0)
    for b in range(COMP):
        stage[b] = sbuf[pl.ds(b, 8, stride=COMP), :]
    for (i, j, c), b in LOWER.items():
        if i % 2 == 0:
            v = sbuf[pl.ds(8 * COMP + b, 8, stride=COMP), :]
            up = LOWER.get((i + 1, j, c))
            up = jnp.zeros((8, 128), F32) if up is None else sbuf[pl.ds(4 * COMP + up, 8, stride=COMP), :]
            stage2[b] = jnp.where(row < 4, v, up)

    def finish(a, v):
        tbuf[pl.ds(a, 8, stride=COMP), :] = v

    def finish2(a, v):
        tbuf[pl.ds(8 * COMP + a, 8, stride=COMP), :] = v + pltpu.roll(v, 4, 0)

    contract(table, h, stage, False, finish, hold, gate)
    contract(table, 2 + h, stage2, True, finish2, hold, gate)


def backward(tbuf, w, turn, ybuf):
    parts = []
    for kc in range(3):
        rows = [(2 * kc + r) * HALF for r in range(2)]
        parts.append(tuple(tbuf[row : row + MROWS, :] for row in rows))
    x = [turned(turn, z, *value, 1.0) for z, value in enumerate(triple(*parts, 1.0))]
    x = jnp.concatenate([jnp.concatenate(v, axis=1) for v in x], axis=0)
    ybuf[...] = product(x, w, 2)


def scatter_columns(ybuf, rest, msg, h, off):
    for r in range(2):
        lanes = slice(128 * r, 128 * r + 128)
        for z in range(ZL):
            at = MROWS * z
            msg[h, pl.ds(2 * z + r, NDEV, stride=8), :] = pltpu.roll(ybuf[at : at + 128, lanes].T, off, 1)
            rest[r, REST * z : REST * z + REST, :] = ybuf[at + 128 : at + HALF, lanes]
        msg[h, pl.ds(6 + r, NDEV, stride=8), :] = pltpu.roll(rest[r].T, off, 1)


def kernel(
    planes_hbm, deriv_hbm, w_hbm, out,
    plane, deriv, w, turn, table, msg, got, msg2, got2, xt, sbuf, stage, stage2, tbuf, hold, ybuf, rest,
    load_sem, own_sem, send_sem, recv_sem, own_sem2, send_sem2, recv_sem2,
):
    me = lax.axis_index("grp") * INNER + lax.axis_index("dev")
    loads = [
        pltpu.make_async_copy(planes_hbm, plane.at[pl.ds(LEAD, ZL * ZROWS), :], load_sem.at[0]),
        pltpu.make_async_copy(deriv_hbm, deriv, load_sem.at[1]),
        pltpu.make_async_copy(w_hbm.at[pl.ds(0, 1072), :], w, load_sem.at[2]),
    ]
    for copy in loads:
        copy.start()
    barrier = pltpu.get_barrier_semaphore()

    each_other(me, lambda d: pl.semaphore_signal(barrier, inc=1, device_id=device(d), device_id_type=MESH))
    plane[0:LEAD, :] = jnp.zeros((LEAD, 128), F32)
    plane[LEAD + ZL * ZROWS :, :] = jnp.zeros((16, 128), F32)
    loads[0].wait()

    for h in range(2):

        @pl.loop(0, NDEV, unroll=8)
        def _(d):
            pack(plane, msg, h, d)

    pl.semaphore_wait(barrier, NDEV - 1)
    for h in range(2):
        send_all(me, msg, got, send_sem, recv_sem, h)
        own_copy(me, msg, got, own_sem, h).start()
    for copy in loads[1:]:
        copy.wait()
    prepare_base(deriv, table)
    prepare_tables(table)
    small = [w[1024 + 16 * n : 1040 + 16 * n, 0:128].astype(F32) for n in range(3)]
    turn[...] = small[0] + (small[1] + small[2])
    xt[...] = jnp.zeros(xt.shape, F32)
    rest[...] = jnp.zeros(rest.shape, F32)
    @pl.loop(0, 2)
    def _(h):
        off = column_start(me, h)[1]
        own_copy(me, msg, got, own_sem, h).wait()
        wait_bytes(got, recv_sem, h)
        gather_columns(got, xt, h, off)
        forward(xt, w, turn, sbuf)
        contract_half(table, h, sbuf, stage, stage2, tbuf, hold, me >= 0)
        backward(tbuf, w, turn, ybuf)
        scatter_columns(ybuf, rest, msg2, h, off)
        send_all(me, msg2, got2, send_sem2, recv_sem2, h)
        own_copy(me, msg2, got2, own_sem2, h).start()

    for h in range(2):
        own_copy(me, msg2, got2, own_sem2, h).wait()
        wait_bytes(got2, recv_sem2, h)

        @pl.loop(0, NDEV, unroll=8)
        def _(s):
            unpack(got2, out, h, s)

    for h in range(2):
        wait_bytes(msg, send_sem, h)
        wait_bytes(msg2, send_sem2, h)


def on_device(multipoles, derivatives):
    planes = with_layout_constraint(multipoles.reshape(2, ZL, COLS, 128), Layout((1, 2, 0, 3)))
    planes = jnp.transpose(planes, (1, 2, 0, 3)).reshape(ZL * ZROWS, 128)
    deriv = jnp.transpose(derivatives, (2, 1, 0))
    vmem, dma = pltpu.VMEM, pltpu.SemaphoreType.DMA
    out = pl.pallas_call(
        kernel,
        out_shape=pltpu.VMEM((OUT_ROWS, 128), F32),
        in_specs=[pl.BlockSpec(memory_space=pl.ANY)] * 3,
        out_specs=pl.BlockSpec(memory_space=pltpu.VMEM),
        scratch_shapes=[
            vmem((PLANE_ROWS, 128), F32),
            vmem((289, 4, NZ), F32),
            vmem((1072, 256), BF16),
            vmem((16, 128), F32),
            vmem((4, PLAN.count, 8, 128), F32),
            vmem((2, 8 * NDEV, 128), F32),
            vmem((2, 8 * NDEV, 128), F32),
            vmem((2, 8 * NDEV, 128), F32),
            vmem((2, 8 * NDEV, 128), F32),
            vmem((ZL * MROWS, 256), F32),
            vmem((16 * COMP, 128), F32),
            vmem((3 * COMP, 8, 128), F32),
            vmem((3 * COMP, 8, 128), F32),
            vmem((16 * COMP, 128), F32),
            vmem((24, 8, 128), F32),
            vmem((ZL * MROWS, 256), F32),
            vmem((2, 128, 128), F32),
            dma((4,)), dma((2,)), dma((2,)), dma((2,)), dma((2,)), dma((2,)), dma((2,)),
        ],
        compiler_params=pltpu.CompilerParams(
            collective_id=0, has_side_effects=True, vmem_limit_bytes=55000000
        ),
        name="m2l",
    )(planes, deriv, jnp.asarray(dft_tables()))
    out = jnp.transpose(out[: ZL * ZROWS].reshape(ZL, COLS, 2, 128), (0, 2, 1, 3)).reshape(ZL, 2, COLS * 128)
    return jnp.transpose(out, (1, 0, 2))


def solution(mesh):
    in_specs = (P(None, ("grp", "dev"), None), P(None, ("grp", "dev"), None))
    out_specs = P(None, ("grp", "dev"), None)
    return jax.shard_map(
        on_device, mesh=mesh, in_specs=in_specs, out_specs=out_specs, check_vma=False
    )
```
